32 devices in a mesh: row: 4 (over y, core), col: 8 (over z, x).
Axes of the slice: x: 2, y: 2, z: 4, core: 2. Of those that a mesh axis runs over, the one named last changes fastest.
Arguments:
- embeddings: float32 [32768, 1024], P(('row', 'col')), may hold values from -6 to 6
- neighbour_ids: int32 [64, 12], P(('row', 'col')), may hold values from 0 to 63, as said below
- start_vectors: float32 [32768, 64], P(('row', 'col')), may hold values from -15 to 15
Outputs:
- spectral_vectors: float32 [32768, 64], P(('row', 'col'))
The draws below stay inside these ranges and needn't reach their ends.
Inputs may be any that keep to these rules, and one draw needn't show every extreme that they name: `neighbour_ids`: slot 0 of block b is b itself. The other slots of block b name distinct blocks other than b held by devices of the same row index whose col index differs from that of b's device by at most 2 cyclically, followed by padding slots that repeat b. Block b sits on device b // 2, with device index row * 8 + col.
All inputs are finite; a program needn't handle non-finite values.
Results may differ from the reference program's by a relative error of at most 0.005.
Values may be sent and summed in bfloat16 or wider, within the bound.
No kernel may reach another device: no remote copies, remote signals or barrier semaphores. Data moves between devices by JAX's collectives and lax.ppermute only.
A program may use at most 128 MiB of HBM per device.

```python
import math
import jax
import jax.numpy as jnp
from jax import lax

D = 1024
BS = 512
SLOTS = 12
K = 64
REACH = 2
ITERS = 3
BLK_DEV = 2
NBLK = 64
NPTS = 32768
N_ROW = 4
N_COL = 8
DEVICES = 32


def draw_embeddings(key, part):
    per_unit = D // 4
    cycle_topics = N_COL * per_unit
    side_topics = 4
    bump_width = 1.5
    row_ids = jnp.arange(NPTS, dtype=jnp.int32)
    holder = row_ids // (BLK_DEV * BS)
    row_of = holder // N_COL
    col_of = holder % N_COL
    topics = jax.random.normal(jax.random.fold_in(key, 21), (N_ROW * cycle_topics, D), jnp.float32)
    anchor = (col_of - 1) * per_unit + jax.random.randint(jax.random.fold_in(key, 22), (NPTS,), 0, 3 * per_unit)
    offset = jax.random.uniform(jax.random.fold_in(key, 23), (NPTS,), jnp.float32, 0.0, 1.0)
    gain_draws = jax.random.uniform(jax.random.fold_in(key, 24), (NPTS, 2 * side_topics + 1), jnp.float32, 0.6, 1.4)
    noise_scale = jax.random.uniform(jax.random.fold_in(key, 25), (NPTS, 1), jnp.float32, 0.25, 0.35)
    noise_draws = jax.random.normal(jax.random.fold_in(key, 26), (NPTS, D), jnp.float32)
    mixture = jnp.zeros((NPTS, D), jnp.float32)
    energy = jnp.zeros((NPTS, 1), jnp.float32)
    for topic_step in range(-side_topics, side_topics + 1):
        topic_index = (row_of * cycle_topics + (anchor + topic_step + cycle_topics) % cycle_topics).astype(jnp.int32)
        distance = topic_step - offset
        weight = (jnp.exp(-distance * distance / (2.0 * bump_width * bump_width)) * gain_draws[:, topic_step + side_topics])[:, None]
        mixture = mixture + weight * topics[topic_index]
        energy = energy + weight * weight
    mixture = mixture / jnp.sqrt(energy) + noise_scale * noise_draws
    mixture = mixture / jnp.sqrt(1.0 + noise_scale * noise_scale)
    return jnp.clip(mixture, -6.0, 6.0)


def draw_neighbour_ids(key, part):
    blocks = jnp.arange(NBLK, dtype=jnp.int32)
    holder = blocks // BLK_DEV
    row_of = holder // N_COL
    col_of = holder % N_COL
    shifts = jnp.repeat(jnp.arange(-REACH, REACH + 1, dtype=jnp.int32), BLK_DEV)
    within = jnp.tile(jnp.arange(BLK_DEV, dtype=jnp.int32), 2 * REACH + 1)
    cand_ids = (row_of[:, None] * N_COL + (col_of[:, None] + shifts[None, :] + N_COL) % N_COL) * BLK_DEV + within[None, :]
    cand_count = (2 * REACH + 1) * BLK_DEV
    scores = jax.random.randint(jax.random.fold_in(key, 1), (NBLK, cand_count), 0, 1 << 20) * cand_count + jnp.arange(cand_count, dtype=jnp.int32)[None, :]
    scores = jnp.where(cand_ids == blocks[:, None], 1 << 30, scores)
    ranking = jnp.argsort(scores, axis=1, stable=True)
    spaces = min(cand_count - 1, SLOTS - 1)
    ranked = jnp.take_along_axis(cand_ids, ranking, axis=1)[:, :spaces]
    device_level = jax.random.randint(jax.random.fold_in(key, 2), (NBLK // BLK_DEV,), 0, 4)
    jitter = jax.random.randint(jax.random.fold_in(key, 3), (NBLK,), 0, 3)
    listed = jnp.clip(1 + 3 * jnp.repeat(device_level, BLK_DEV) + jitter, 1, spaces)
    listed = listed.at[0].set(spaces)
    listed_ids = jnp.where(jnp.arange(spaces)[None, :] < listed[:, None], ranked, blocks[:, None])
    padding = jnp.broadcast_to(blocks[:, None], (NBLK, SLOTS - 1 - spaces))
    return jnp.concatenate([blocks[:, None], listed_ids, padding], axis=1).astype(jnp.int32)


def draw_start_vectors(key, part):
    row_ids = jnp.arange(NPTS, dtype=jnp.int32)
    device_rise = 1.0 + 2.0 * (row_ids // (BLK_DEV * BS)).astype(jnp.float32) / max(DEVICES - 1, 1)
    values = jnp.clip(jax.random.normal(key, (NPTS, K), jnp.float32), -5.0, 5.0)
    return values * device_rise[:, None]


def setup_inputs(seed: int = 0) -> dict:
    splits = jax.random.split(jax.random.key(seed), 4)
    return {
        "embeddings": draw_embeddings(jax.random.fold_in(splits[3], 71), 0),
        "neighbour_ids": draw_neighbour_ids(jax.random.fold_in(splits[3], 71), 0),
        "start_vectors": draw_start_vectors(jax.random.fold_in(splits[3], 71), 0),
    }


SHARP = 8.0
EPSILON = 1e-06

def unit_rows(points):
    rms_inverse = lax.rsqrt(lax.optimization_barrier(jnp.mean(points * points, axis=-1, keepdims=True)) + EPSILON)
    return (points * rms_inverse).astype(jnp.bfloat16)

def orthonormal(image_rows, total_rows):
    gram_sum = lax.dot_general(image_rows.astype(jnp.float32), image_rows.astype(jnp.float32), (((0,), (0,)), ((), ())), precision=lax.Precision.HIGHEST, preferred_element_type=jnp.float32)
    factor = jnp.linalg.cholesky(gram_sum)
    solved = lax.linalg.triangular_solve(factor, image_rows, left_side=False, lower=True, transpose_a=True)
    return solved * math.sqrt(total_rows)

def reference(embeddings, neighbour_ids, start_vectors):
    block_count = neighbour_ids.shape[0]
    normed = unit_rows(embeddings).reshape(block_count, BS, D)
    block_ids = jnp.arange(block_count, dtype=jnp.int32)
    slot_ids = jnp.arange(SLOTS, dtype=jnp.int32)
    live_mask = ((slot_ids[None, :] == 0) | (neighbour_ids != block_ids[:, None])).astype(jnp.float32)

    def tiles_of(packed):
        own_rows, block_list, live_rows = packed
        nearby = normed[block_list].astype(jnp.float32)
        cosine = jnp.einsum('pd,kqd->kpq', own_rows.astype(jnp.float32), nearby) / D
        affinity = jnp.exp(SHARP * (cosine - 1.0)) * live_rows[:, None, None]
        degree = lax.optimization_barrier(jnp.sum(affinity, axis=(0, 2)))
        return (affinity.astype(jnp.bfloat16), degree)
    tile_rows, degree = lax.map(tiles_of, (normed, neighbour_ids, live_mask))
    inv_root = lax.rsqrt(degree)
    vectors = start_vectors
    for iteration in range(ITERS):
        scaled = (vectors * inv_root.reshape(-1, 1)).astype(jnp.bfloat16).reshape(block_count, BS, K)

        def apply(packed):
            tile_block, block_list, root_rows = packed
            nearby = scaled[block_list].astype(jnp.float32)
            return jnp.einsum('kpq,kqc->pc', tile_block.astype(jnp.float32), nearby) * root_rows[:, None]
        image_rows = lax.map(apply, (tile_rows, neighbour_ids, inv_root)).reshape(-1, K)
        vectors = orthonormal(image_rows, NPTS)
    return vectors
```

```python
import math

import jax
import jax.numpy as jnp
from jax import lax
from jax.sharding import PartitionSpec as P

D = 1024
BS = 512
SLOTS = 12
REACH = 2
ITERS = 3
BLK_DEV = 2


SHARP = 8.0
EPSILON = 1e-06


def passed_along(shard, axis, by):
    count = lax.axis_size(axis)
    return lax.ppermute(shard, axis, [(i, (i + by) % count) for i in range(count)])


def unit_rows(points):
    rms_inverse = lax.rsqrt(jnp.mean(points * points, axis=-1, keepdims=True) + EPSILON)
    return (points * rms_inverse).astype(jnp.bfloat16)


def band_index(neighbour_ids, col_count, col_index):
    holder = neighbour_ids // BLK_DEV
    offset = (holder % col_count - col_index + col_count + REACH) % col_count
    return offset * BLK_DEV + neighbour_ids % BLK_DEV


def assemble(pieces):
    return jnp.concatenate([pieces[offset] for offset in range(-REACH, REACH + 1)], axis=0)


def point_band(normed):
    pieces = {0: normed}
    for offset in [shifted for shifted in range(-REACH, REACH + 1) if shifted != 0]:
        pieces[offset] = passed_along(normed, "col", -offset)
    return assemble(pieces)


def vector_band(scaled):
    pieces = {0: scaled}
    for offset in [shifted for shifted in range(-REACH, REACH + 1) if shifted != 0]:
        pieces[offset] = passed_along(scaled, "col", -offset)
    return assemble(pieces)


def exchange_masks(row_count, col_count):
    low = [1 << bit for bit in range(col_count.bit_length() - 1)]
    high = [col_count << bit for bit in range(row_count.bit_length() - 1)]
    stages = [(high[0],), (high[1], low[0]), (low[1], low[2])]
    rest = high[2:] + low[3:]
    return stages + [tuple(rest[at : at + 2]) for at in range(0, len(rest), 2)]


def total_sum(value):
    row_count = lax.axis_size("row")
    col_count = lax.axis_size("col")
    devices = row_count * col_count
    if devices & (devices - 1) or row_count < 4 or col_count < 8:
        return lax.psum(value, ("row", "col"))

    def fetched(mask):
        pairs = [(source, source ^ mask) for source in range(devices)]
        return lax.ppermute(value, ("row", "col"), pairs)

    for masks in exchange_masks(row_count, col_count):
        if len(masks) == 1:
            value = value + fetched(masks[0])
        else:
            first, second = masks
            near, far, both = fetched(first), fetched(second), fetched(first ^ second)
            value = (value + near) + (far + both)
    return value


def orthonormal(image_rows, total_rows):
    gram_sum = lax.dot_general(
        image_rows,
        image_rows,
        (((0,), (0,)), ((), ())),
        precision=lax.Precision.HIGHEST,
        preferred_element_type=jnp.float32,
    )
    gram_sum = total_sum(gram_sum)
    factor = jnp.linalg.cholesky(gram_sum)
    solved = lax.linalg.triangular_solve(
        factor, image_rows, left_side=False, lower=True, transpose_a=True
    )
    return solved * math.sqrt(total_rows)


def on_device(embeddings, neighbour_ids, start_vectors):
    col_count = lax.axis_size("col")
    col_index = lax.axis_index("col")
    device = lax.axis_index("row") * col_count + col_index
    total_rows = embeddings.shape[0] * lax.axis_size("row") * col_count
    normed = unit_rows(embeddings)
    point_rows = point_band(normed)
    own_ids = device * BLK_DEV + jnp.arange(BLK_DEV, dtype=jnp.int32)
    slot_ids = jnp.arange(SLOTS, dtype=jnp.int32)
    live_mask = ((slot_ids[None, :] == 0) | (neighbour_ids != own_ids[:, None])).astype(jnp.float32)
    position = band_index(neighbour_ids, col_count, col_index)
    candidates = (2 * REACH + 1) * BLK_DEV
    own_blocks = normed.reshape(BLK_DEV, BS, D)
    tile_list = []
    degree_list = []
    chosen = jnp.sum(
        (position[:, :, None] == jnp.arange(candidates, dtype=jnp.int32)[None, None, :]).astype(
            jnp.float32
        )
        * live_mask[:, :, None],
        axis=1,
    )
    for member in range(BLK_DEV):
        cosine = (
            lax.dot_general(
                own_blocks[member],
                point_rows,
                (((1,), (1,)), ((), ())),
                preferred_element_type=jnp.float32,
            )
            / D
        )
        affinity = (
            jnp.exp(SHARP * (cosine - 1.0)).reshape(BS, candidates, BS)
            * chosen[member][None, :, None]
        )
        degree_list.append(jnp.sum(affinity, axis=(1, 2)))
        tile_list.append(affinity.reshape(BS, candidates * BS).astype(jnp.bfloat16))
    inv_root = lax.rsqrt(jnp.stack(degree_list))
    vectors = start_vectors
    for iteration in range(ITERS):
        scaled = (vectors * inv_root.reshape(-1, 1)).astype(jnp.bfloat16)
        spread = vector_band(scaled)
        image_list = []
        for member in range(BLK_DEV):
            partial_rows = jnp.dot(tile_list[member], spread, preferred_element_type=jnp.float32)
            image_list.append(partial_rows * inv_root[member][:, None])
        image_rows = jnp.concatenate(image_list, axis=0)
        vectors = orthonormal(image_rows, total_rows)
    return vectors


def solution(mesh):
    in_specs = (P(("row", "col"), None), P(("row", "col"), None), P(("row", "col"), None))
    out_specs = P(("row", "col"), None)
    return jax.shard_map(
        on_device, mesh=mesh, in_specs=in_specs, out_specs=out_specs, check_vma=False
    )
```

```python
import functools
import math

import jax
import jax.numpy as jnp
from jax import lax
from jax.experimental import pallas as pl
from jax.experimental.pallas import tpu as pltpu
from jax.sharding import PartitionSpec as P

REACH = 2
ITERS = 3
BLK_DEV = 2

SHARP = 8.0
EPSILON = 1e-06

F32 = jnp.float32
BF16 = jnp.bfloat16
EXACT = lax.Precision.HIGHEST
VMEM = pl.BlockSpec(memory_space=pltpu.VMEM)
SMEM = pl.BlockSpec(memory_space=pltpu.SMEM)


def call(body, out_shape, in_specs, name, flops, moved):
    return pl.pallas_call(
        body,
        out_shape=out_shape,
        in_specs=in_specs,
        out_specs=jax.tree.map(lambda _: VMEM, out_shape),
        cost_estimate=pl.CostEstimate(flops=flops, bytes_accessed=moved, transcendentals=0),
        compiler_params=pltpu.CompilerParams(vmem_limit_bytes=56 << 20),
        name=name,
    )


def shaped(shape, dtype):
    return jax.ShapeDtypeStruct(shape, dtype)


def cross(left, right, **kw):
    return lax.dot_general(
        left, right, (((1,), (1,)), ((), ())), preferred_element_type=F32, **kw
    )


def unit_rows_body(points_ref, out_ref):
    points = points_ref[...]
    mean = jnp.mean(points * points, axis=-1, keepdims=True)
    out_ref[...] = (points * lax.rsqrt(mean + EPSILON)).astype(BF16)


def unit_rows(points, block, size):
    width = points.shape[1]
    step = 128
    per = size // step
    return pl.pallas_call(
        unit_rows_body,
        grid=(per,),
        in_specs=[pl.BlockSpec((step, width), lambda i: (block * per + i, 0))],
        out_specs=pl.BlockSpec((step, width), lambda i: (i, 0)),
        out_shape=shaped((size, width), BF16),
        cost_estimate=pl.CostEstimate(
            flops=3 * size * width, bytes_accessed=6 * size * width, transcendentals=0
        ),
        name="unit_rows",
    )(points)


def affinity(rows, cols):
    width = rows.shape[1]
    return jnp.exp(cross(rows, cols) * (SHARP / width) - SHARP)


def down(tile):
    return jnp.sum(tile, axis=0, keepdims=True)


def across(tile):
    lanes = 128
    folded = tile[:, :lanes]
    for at in range(lanes, tile.shape[1], lanes):
        folded = folded + tile[:, at : at + lanes]
    return jnp.sum(folded.T, axis=0, keepdims=True)


def own_tiles_body(b0, b1, oo, sums):
    size = b0.shape[0]
    for l, rows in enumerate((b0, b1)):
        for m, cols in enumerate((b0, b1)):
            tile = affinity(rows[...], cols[...])
            oo[l * size : (l + 1) * size, m * size : (m + 1) * size] = tile.astype(BF16)
            sums[l : l + 1, m * size : (m + 1) * size] = down(tile)


def row_tiles(rows, owns, out, sums):
    size = rows.shape[0]
    for m, cols in enumerate(owns):
        tile = affinity(rows[...], cols[...])
        out[:, m * size : (m + 1) * size] = tile.astype(BF16)
        sums[:, m * size : (m + 1) * size] = down(tile)


def col_tiles(owns, cols, out, sums, side):
    size = cols.shape[0]
    for l, rows in enumerate(owns):
        tile = affinity(rows[...], cols[...])
        out[l * size : (l + 1) * size, :] = tile.astype(BF16)
        sums[l : l + 1, :] = down(tile)
        side[:, l * size : (l + 1) * size] = across(tile)


def one_tile(rows, cols, out, sums):
    tile = affinity(rows[...], cols[...])
    out[...] = tile.astype(BF16)
    sums[...] = down(tile)


def first_tiles_body(b0, b1, x0, z0, x0o, x0o_s, oz0, oz0_s, oz0_r, x0z0, x0z0_s):
    row_tiles(x0, (b0, b1), x0o, x0o_s)
    col_tiles((b0, b1), z0, oz0, oz0_s, oz0_r)
    one_tile(x0, z0, x0z0, x0z0_s)


def last_tiles_body(
    b0, b1, x0, x1, z0, z1,
    x1o, x1o_s, oz1, oz1_s, oz1_r, x1z0, x1z0_s, x0z1, x0z1_s, x1z1, x1z1_s,
):
    row_tiles(x1, (b0, b1), x1o, x1o_s)
    one_tile(x1, z0, x1z0, x1z0_s)
    col_tiles((b0, b1), z1, oz1, oz1_s, oz1_r)
    one_tile(x0, z1, x0z1, x0z1_s)
    one_tile(x1, z1, x1z1, x1z1_s)


def kept(vectors, mask):
    return jnp.where(mask > 0.0, vectors, jnp.zeros_like(vectors))


def far_rows_body(mask, own, x, oz0, oz1, x0z0, x1z0, x0z1, x1z1, out):
    size = x0z0.shape[0]
    for m, (oz, xz) in enumerate(((oz0, (x0z0, x1z0)), (oz1, (x0z1, x1z1)))):
        total = None
        for l in range(BLK_DEV):
            here = slice(l * size, (l + 1) * size)
            part = jnp.dot(kept(own[:, here], mask[m, l]), oz[here, :], preferred_element_type=F32)
            part += jnp.dot(
                kept(x[:, here], mask[m, BLK_DEV + l]), xz[l][...], preferred_element_type=F32
            )
            total = part if total is None else total + part
        out[:, m * size : (m + 1) * size] = total


def own_rows_body(mask, own, x, z, given, root, oo, x0o, x1o, oz0, oz1, image, gram):
    size = x0o.shape[0]
    for m in range(BLK_DEV):
        there = slice(m * size, (m + 1) * size)
        total = given[:, there]
        for l, (xo, oz) in enumerate(((x0o, oz0), (x1o, oz1))):
            here = slice(l * size, (l + 1) * size)
            total += jnp.dot(
                kept(own[:, here], mask[m, l]), oo[here, there], preferred_element_type=F32
            )
            total += jnp.dot(
                kept(x[:, here], mask[m, BLK_DEV + l]), xo[:, there], preferred_element_type=F32
            )
            total += cross(kept(z[:, here], mask[m, 2 * BLK_DEV + l]), oz[there, :])
        image[:, there] = total * root[:, there]
    full = image[...]
    gram[...] = cross(full, full, precision=EXACT)


def inverse_factor(gram):
    size = gram.shape[0]
    rows = lax.broadcasted_iota(jnp.int32, (size, 2 * size), 0)
    lanes = lax.broadcasted_iota(jnp.int32, (size, 2 * size), 1)
    unit = jnp.where(rows + size == lanes, 1.0, 0.0).astype(F32)
    work = jnp.concatenate([gram, unit[:, size:]], axis=1)
    for j in range(size):
        pivot_row = work[j : j + 1, :]
        scale = 1.0 / pivot_row[:, j : j + 1]
        factor = jnp.where(rows[:, :1] > j, work[:, j : j + 1] * scale, 0.0)
        work = work - factor * pivot_row
    diagonal = jnp.sum(jnp.where(rows == lanes, work, 0.0), axis=1, keepdims=True)
    return work[:, size:] * lax.rsqrt(diagonal)


def solve_body(scale, gram, image, root, out, scaled):
    factor = inverse_factor(gram[...])
    vectors = jnp.dot(factor, image[...], preferred_element_type=F32, precision=EXACT) * scale
    out[...] = vectors
    scaled[...] = (vectors * root[...]).astype(BF16)


def exchange_masks(row_count, col_count):
    low = [1 << bit for bit in range(col_count.bit_length() - 1)]
    high = [col_count << bit for bit in range(row_count.bit_length() - 1)]
    stages = [(high[0],), (high[1], low[0]), (low[1], low[2])]
    rest = high[2:] + low[3:]
    return stages + [tuple(rest[at : at + 2]) for at in range(0, len(rest), 2)]


def total_sum(value):
    row_count = lax.axis_size("row")
    col_count = lax.axis_size("col")
    devices = row_count * col_count
    if devices & (devices - 1) or row_count < 4 or col_count < 8:
        return lax.psum(value, ("row", "col"))

    def fetched(mask):
        pairs = [(source, source ^ mask) for source in range(devices)]
        return lax.ppermute(value, ("row", "col"), pairs)

    for masks in exchange_masks(row_count, col_count):
        if len(masks) == 1:
            value = value + fetched(masks[0])
        else:
            first, second = masks
            near, far, both = fetched(first), fetched(second), fetched(first ^ second)
            value = (value + near) + (far + both)
    return value


def on_device(embeddings, neighbour_ids, start_vectors):
    col_count = lax.axis_size("col")
    col = lax.axis_index("col")
    base = lax.axis_index("row") * col_count
    points, width = embeddings.shape
    columns = start_vectors.shape[1]
    size = points // BLK_DEV
    total_rows = points * lax.axis_size("row") * col_count

    def side_of(index):
        return (index + (REACH if index % 2 == 0 else -REACH)) % col_count

    def from_x(value):
        return lax.ppermute(value, "col", [(i, i ^ 1) for i in range(col_count)])

    def from_z(value):
        return lax.ppermute(value, "col", [(side_of(i), i) for i in range(col_count)])

    def to_z(value):
        return lax.ppermute(value, "col", [(i, side_of(i)) for i in range(col_count)])

    b0 = unit_rows(embeddings, 0, size)
    z0 = from_z(b0)
    x0 = from_x(b0)
    b1 = unit_rows(embeddings, 1, size)
    z1 = from_z(b1)
    x1 = from_x(b1)
    far_ids = from_z(neighbour_ids)

    here = base + col
    x_side = base + (col ^ 1)
    z_side = base + (col + jnp.where(col % 2 == 0, REACH, col_count - REACH)) % col_count
    members = jnp.arange(BLK_DEV, dtype=jnp.int32)
    near = jnp.stack([here, x_side, z_side])[:, None] * BLK_DEV + members[None, :]
    near = near.reshape(-1)
    own_mask = jnp.max((neighbour_ids[:, :, None] == near[None, None, :]).astype(F32), axis=1)
    far_mask = jnp.max(
        (far_ids[:, :, None] == near[None, None, : 2 * BLK_DEV]).astype(F32), axis=1
    )

    half, tile = shaped((size, points), BF16), shaped((size, size), BF16)
    tall = shaped((points, size), BF16)
    line, short = shaped((1, points), F32), shaped((1, size), F32)
    two, pair = shaped((BLK_DEV, points), F32), shaped((BLK_DEV, size), F32)
    square = shaped((points, points), BF16)
    one = 2 * size * size * width
    moved = 4 * size * width
    oo, oo_s = call(own_tiles_body, (square, two), [VMEM] * 2, "own_tiles", 4 * one, 4 * moved)(
        b0, b1
    )
    x0o, x0o_s, oz0, oz0_s, oz0_r, x0z0, x0z0_s = call(
        first_tiles_body,
        (half, line, tall, pair, line, tile, short),
        [VMEM] * 4, "first_tiles", 5 * one, 5 * moved,
    )(b0, b1, x0, z0)
    x1o, x1o_s, oz1, oz1_s, oz1_r, x1z0, x1z0_s, x0z1, x0z1_s, x1z1, x1z1_s = call(
        last_tiles_body,
        (half, line, tall, pair, line, tile, short, tile, short, tile, short),
        [VMEM] * 6, "last_tiles", 7 * one, 7 * moved,
    )(b0, b1, x0, x1, z0, z1)

    lanes = jnp.repeat(own_mask.T, size, axis=1)
    sums = jnp.concatenate([oo_s, x0o_s, x1o_s, oz0_r, oz1_r], axis=0)
    own_degree = jnp.sum(jnp.where(lanes > 0, sums, 0.0), axis=0, keepdims=True)
    far_lanes = jnp.repeat(far_mask.T, size, axis=1)
    far_sums = jnp.concatenate(
        [
            jnp.concatenate([oz0_s, x0z0_s, x1z0_s], axis=0),
            jnp.concatenate([oz1_s, x0z1_s, x1z1_s], axis=0),
        ],
        axis=1,
    )
    far_degree = jnp.sum(jnp.where(far_lanes > 0, far_sums, 0.0), axis=0, keepdims=True)
    root = lax.rsqrt(own_degree + to_z(far_degree))

    across_shape = (columns, points)
    work = 2 * columns * size * size
    far_rows = call(
        far_rows_body, shaped(across_shape, F32), [SMEM] + [VMEM] * 8, "far_rows", 8 * work, 8 * work // 64
    )
    own_rows = call(
        own_rows_body,
        (shaped(across_shape, F32), shaped((columns, columns), F32)),
        [SMEM] + [VMEM] * 10, "own_rows", 12 * work, 12 * work // 64,
    )
    solve = call(
        functools.partial(solve_body, math.sqrt(total_rows)),
        (shaped(across_shape, F32), shaped(across_shape, BF16)),
        [VMEM] * 3, "solve", 4 * columns * columns * points, 4 * columns * points,
    )
    vectors = start_vectors.T
    scaled = (vectors * root).astype(BF16)
    for iteration in range(ITERS):
        x = from_x(scaled)
        z = from_z(scaled)
        given = to_z(far_rows(far_mask, scaled, x, oz0, oz1, x0z0, x1z0, x0z1, x1z1))
        image, gram = own_rows(own_mask, scaled, x, z, given, root, oo, x0o, x1o, oz0, oz1)
        vectors, scaled = solve(total_sum(gram), image, root)
    return vectors.T


def solution(mesh):
    in_specs = (P(("row", "col"), None), P(("row", "col"), None), P(("row", "col"), None))
    out_specs = P(("row", "col"), None)
    return jax.shard_map(
        on_device, mesh=mesh, in_specs=in_specs, out_specs=out_specs, check_vma=False
    )
```

```python
import functools
import math

import jax
import jax.numpy as jnp
from jax import lax
from jax.experimental import pallas as pl
from jax.experimental.pallas import tpu as pltpu
from jax.sharding import PartitionSpec as P

REACH = 2
ITERS = 3
BLK_DEV = 2

SHARP = 8.0
EPSILON = 1e-06

F32 = jnp.float32
BF16 = jnp.bfloat16
EXACT = lax.Precision.HIGHEST
VMEM = pl.BlockSpec(memory_space=pltpu.VMEM)
SMEM = pl.BlockSpec(memory_space=pltpu.SMEM)


def call(body, out_shape, in_specs, flops, moved, room=6, aliases=None):
    return pl.pallas_call(
        body,
        out_shape=out_shape,
        in_specs=in_specs,
        out_specs=jax.tree.map(lambda _: VMEM, out_shape),
        input_output_aliases=aliases or {},
        cost_estimate=pl.CostEstimate(flops=flops, bytes_accessed=moved, transcendentals=0),
        compiler_params=pltpu.CompilerParams(vmem_limit_bytes=room << 20),
    )


def shaped(shape, dtype):
    return jax.ShapeDtypeStruct(shape, dtype)


def cross(left, right, **kw):
    return lax.dot_general(
        left, right, (((1,), (1,)), ((), ())), preferred_element_type=F32, **kw
    )


STEPS = 8


def unit_rows_body(block, points_ref, out_ref, held, arrived):
    size = out_ref.shape[0]
    step = size // STEPS
    copies = []
    for at in range(STEPS):
        rows = pl.ds(at * step, step)
        source = points_ref.at[pl.ds(block * size + at * step, step)]
        copies.append(pltpu.make_async_copy(source, held.at[rows], arrived.at[at]))
        copies[-1].start()
    for at in range(STEPS):
        copies[at].wait()
        rows = pl.ds(at * step, step)
        points = held[rows, :]
        mean = jnp.mean(points * points, axis=-1, keepdims=True)
        out_ref[rows, :] = (points * lax.rsqrt(mean + EPSILON)).astype(BF16)


def unit_rows(points, block, size):
    width = points.shape[1]
    return pl.pallas_call(
        functools.partial(unit_rows_body, block),
        in_specs=[pl.BlockSpec(memory_space=pltpu.HBM)],
        out_specs=VMEM,
        out_shape=shaped((size, width), BF16),
        scratch_shapes=[pltpu.VMEM((size, width), F32), pltpu.SemaphoreType.DMA((STEPS,))],
        cost_estimate=pl.CostEstimate(
            flops=3 * size * width, bytes_accessed=6 * size * width, transcendentals=0
        ),
        compiler_params=pltpu.CompilerParams(vmem_limit_bytes=61 << 20),
        name="unit_rows",
    )(points)


def affinity(rows, cols):
    width = rows.shape[1]
    return jnp.exp(cross(rows, cols) * (SHARP / width) - SHARP)


def down(tile):
    return jnp.sum(tile, axis=0, keepdims=True)


def across(tile):
    lanes = 128
    folded = tile[:, :lanes]
    for at in range(lanes, tile.shape[1], lanes):
        folded = folded + tile[:, at : at + lanes]
    return jnp.sum(folded.T, axis=0, keepdims=True)


def gated(mask, sums):
    return jnp.where(mask > 0.0, sums, 0.0)


def span(index, size):
    return slice(index * size, (index + 1) * size)


def x_own(own_mask, l, x, owns, near, first, degree):
    size = x.shape[0]
    for m, cols in enumerate(owns):
        tile = affinity(x[...], cols[...])
        near[span(l - first, size), span(m, size)] = tile.astype(BF16)
        degree[:, span(m, size)] += gated(own_mask[m, l], down(tile))


def own_z(own_mask, owns, m, z, far, degree):
    size = z.shape[0]
    sums = []
    for l, rows in enumerate(owns):
        tile = affinity(rows[...], z[...])
        far[span(l, size), :] = tile.astype(BF16)
        degree[:, span(l, size)] += gated(own_mask[l, 2 * BLK_DEV + m], across(tile))
        sums.append(down(tile))
    return sums


def x_z(x, z, far, at):
    tile = affinity(x[...], z[...])
    far[span(at, z.shape[0]), :] = tile.astype(BF16)
    return down(tile)


def first_tiles_body(own_mask, b0, b1, x0, z0, near, far, degree, far_sums):
    degree[...] = jnp.zeros_like(degree)
    for l, rows in enumerate((b0, b1, x0)):
        x_own(own_mask, l, rows, (b0, b1), near, 0, degree)
    sums = own_z(own_mask, (b0, b1), 0, z0, far, degree)
    sums.append(x_z(x0, z0, far, BLK_DEV))
    for l, line in enumerate(sums):
        far_sums[l : l + 1, :] = line


def last_tiles_body(
    own_mask, far_mask, b0, b1, x0, x1, z0, z1, degree_in, far_sums,
    near, corner, far, degree, far_degree,
):
    size = z0.shape[0]
    degree[...] = degree_in[...]
    x_own(own_mask, BLK_DEV + 1, x1, (b0, b1), near, BLK_DEV + 1, degree)
    early = [far_sums[l : l + 1, :] for l in range(far_sums.shape[0])]
    early.append(x_z(x1, z0, corner, 0))
    late = own_z(own_mask, (b0, b1), 1, z1, far, degree)
    late.append(x_z(x0, z1, far, BLK_DEV))
    late.append(x_z(x1, z1, far, BLK_DEV + 1))
    for m, sums in enumerate((early, late)):
        total = jnp.zeros((1, size), F32)
        for l, line in enumerate(sums):
            total += gated(far_mask[m, l], line)
        far_degree[:, span(m, size)] = total


def kept(mask, m, first, *vectors):
    parts = []
    at = first
    for value in vectors:
        size = value.shape[1] // BLK_DEV
        for l in range(BLK_DEV):
            part = value[:, span(l, size)]
            parts.append(jnp.where(mask[m, at] > 0.0, part, jnp.zeros_like(part)))
            at += 1
    return jnp.concatenate(parts, axis=1)


def apart(left, right):
    return jnp.dot(left, right, preferred_element_type=F32)


def far_rows_body(mask, own, x, far0, corner, far1, out):
    size = own.shape[1] // BLK_DEV
    cut = far0.shape[0]
    left = kept(mask, 0, 0, own, x)
    out[:, span(0, size)] = apart(left[:, :cut], far0[...]) + apart(left[:, cut:], corner[...])
    out[:, span(1, size)] = apart(kept(mask, 1, 0, own, x), far1[...])


def own_rows_body(mask, own, x, z, given, root, near0, near1, far0, far1, image, gram):
    size = own.shape[1] // BLK_DEV
    cut = near0.shape[0]
    for m in range(BLK_DEV):
        there = span(m, size)
        left = kept(mask, m, 0, own, x)
        side = kept(mask, m, 2 * BLK_DEV, z)
        total = given[:, there] + apart(left[:, :cut], near0[:, there])
        total += apart(left[:, cut:], near1[:, there])
        total += cross(side[:, :size], far0[there, :]) + cross(side[:, size:], far1[there, :])
        image[:, there] = total * root[:, there]
    full = image[...]
    gram[...] = cross(full, full, precision=EXACT)


def inverse_factor(gram):
    size = gram.shape[0]
    rows = lax.broadcasted_iota(jnp.int32, (size, 2 * size), 0)
    lanes = lax.broadcasted_iota(jnp.int32, (size, 2 * size), 1)
    unit = jnp.where(rows + size == lanes, 1.0, 0.0).astype(F32)
    work = jnp.concatenate([gram, unit[:, size:]], axis=1)
    for j in range(size):
        pivot_row = work[j : j + 1, :]
        scale = 1.0 / pivot_row[:, j : j + 1]
        factor = jnp.where(rows[:, :1] > j, work[:, j : j + 1] * scale, 0.0)
        work = work - factor * pivot_row
    diagonal = jnp.sum(jnp.where(rows == lanes, work, 0.0), axis=1, keepdims=True)
    return work[:, size:] * lax.rsqrt(diagonal)


def solve_body(scale, gram, image, root, out, scaled):
    factor = inverse_factor(gram[...])
    vectors = jnp.dot(factor, image[...], preferred_element_type=F32, precision=EXACT) * scale
    out[...] = vectors
    scaled[...] = (vectors * root[...]).astype(BF16)


def exchange_masks(row_count, col_count):
    low = [1 << bit for bit in range(col_count.bit_length() - 1)]
    high = [col_count << bit for bit in range(row_count.bit_length() - 1)]
    stages = [(high[0],), (high[1], low[0]), (low[1], low[2])]
    rest = high[2:] + low[3:]
    return stages + [tuple(rest[at : at + 2]) for at in range(0, len(rest), 2)]


def total_sum(value):
    row_count = lax.axis_size("row")
    col_count = lax.axis_size("col")
    devices = row_count * col_count
    if devices & (devices - 1) or row_count < 4 or col_count < 8:
        return lax.psum(value, ("row", "col"))

    def fetched(mask):
        pairs = [(source, source ^ mask) for source in range(devices)]
        return lax.ppermute(value, ("row", "col"), pairs)

    for masks in exchange_masks(row_count, col_count):
        if len(masks) == 1:
            value = value + fetched(masks[0])
        else:
            first, second = masks
            near, far, both = fetched(first), fetched(second), fetched(first ^ second)
            value = (value + near) + (far + both)
    return value


def listed(ids, blocks):
    found = jnp.zeros((ids.shape[0], blocks.shape[0]), bool)
    for slot in range(ids.shape[1]):
        found = found | (ids[:, slot : slot + 1] == blocks[None, :])
    return found.astype(F32)


def on_device(embeddings, neighbour_ids, start_vectors):
    col_count = lax.axis_size("col")
    col = lax.axis_index("col")
    base = lax.axis_index("row") * col_count
    points, width = embeddings.shape
    columns = start_vectors.shape[1]
    size = points // BLK_DEV
    total_rows = points * lax.axis_size("row") * col_count

    def side_of(index):
        return (index + (REACH if index % 2 == 0 else -REACH)) % col_count

    def from_x(value):
        return lax.ppermute(value, "col", [(i, i ^ 1) for i in range(col_count)])

    def from_z(value):
        return lax.ppermute(value, "col", [(side_of(i), i) for i in range(col_count)])

    def to_z(value):
        return lax.ppermute(value, "col", [(i, side_of(i)) for i in range(col_count)])

    b0 = unit_rows(embeddings, 0, size)
    z0 = from_z(b0)
    x0 = from_x(b0)
    b1 = unit_rows(embeddings, 1, size)
    z1 = from_z(b1)
    x1 = from_x(b1)
    far_ids = from_z(neighbour_ids)

    here = base + col
    x_side = base + (col ^ 1)
    z_side = base + (col + jnp.where(col % 2 == 0, REACH, col_count - REACH)) % col_count
    members = jnp.arange(BLK_DEV, dtype=jnp.int32)
    nearby = jnp.stack([here, x_side, z_side])[:, None] * BLK_DEV + members[None, :]
    nearby = nearby.reshape(-1)
    own_mask = listed(neighbour_ids, nearby)
    far_mask = listed(far_ids, nearby[: 2 * BLK_DEV])

    line = shaped((1, points), F32)
    one = 2 * size * size * width
    moved = 4 * size * width
    most = 2 * BLK_DEV - 1
    near0, far0, degree, far_sums = call(
        first_tiles_body,
        (
            shaped((most * size, points), BF16), shaped((most * size, size), BF16), line,
            shaped((most, size), F32),
        ),
        [SMEM] + [VMEM] * 4, 9 * one, 9 * moved,
    )(own_mask, b0, b1, x0, z0)
    near1, corner, far1, degree, far_degree = call(
        last_tiles_body,
        (
            shaped((size, points), BF16), shaped((size, size), BF16),
            shaped((2 * points, size), BF16), line, line,
        ),
        [SMEM] * 2 + [VMEM] * 8, 7 * one, 7 * moved,
    )(own_mask, far_mask, b0, b1, x0, x1, z0, z1, degree, far_sums)
    root = lax.rsqrt(degree + to_z(far_degree))

    across_shape = (columns, points)
    work = 2 * columns * size * size
    far_rows = call(
        far_rows_body, shaped(across_shape, F32), [SMEM] + [VMEM] * 5, 8 * work, 8 * work // 64
    )
    own_rows = call(
        own_rows_body,
        (shaped(across_shape, F32), shaped((columns, columns), F32)),
        [SMEM] + [VMEM] * 9, 12 * work, 12 * work // 64,
    )
    solve = call(
        functools.partial(solve_body, math.sqrt(total_rows)),
        (shaped(across_shape, F32), shaped(across_shape, BF16)),
        [VMEM] * 3, 4 * columns * columns * points, 4 * columns * points,
    )
    vectors = start_vectors.T
    scaled = (vectors * root).astype(BF16)
    for _ in range(ITERS):
        x = from_x(scaled)
        z = from_z(scaled)
        given = to_z(far_rows(far_mask, scaled, x, far0, corner, far1))
        image, gram = own_rows(own_mask, scaled, x, z, given, root, near0, near1, far0, far1)
        vectors, scaled = solve(total_sum(gram), image, root)
    return vectors.T


def solution(mesh):
    in_specs = (P(("row", "col"), None), P(("row", "col"), None), P(("row", "col"), None))
    out_specs = P(("row", "col"), None)
    return jax.shard_map(on_device, mesh=mesh, in_specs=in_specs, out_specs=out_specs, check_vma=False)
```

```python
import functools
import math

import jax
import jax.numpy as jnp
from jax import lax
from jax.experimental import pallas as pl
from jax.experimental.pallas import tpu as pltpu
from jax.sharding import PartitionSpec as P

REACH = 2
ITERS = 3
BLK_DEV = 2

SHARP = 8.0
EPSILON = 1e-06

F32 = jnp.float32
BF16 = jnp.bfloat16
EXACT = lax.Precision.HIGHEST
VMEM = pl.BlockSpec(memory_space=pltpu.VMEM)
SMEM = pl.BlockSpec(memory_space=pltpu.SMEM)


def call(body, out_shape, in_specs, flops, moved, room=6, aliases=None):
    return pl.pallas_call(
        body,
        out_shape=out_shape,
        in_specs=in_specs,
        out_specs=jax.tree.map(lambda _: VMEM, out_shape),
        input_output_aliases=aliases or {},
        cost_estimate=pl.CostEstimate(flops=flops, bytes_accessed=moved, transcendentals=0),
        compiler_params=pltpu.CompilerParams(vmem_limit_bytes=room << 20),
    )


def shaped(shape, dtype):
    return jax.ShapeDtypeStruct(shape, dtype)


def cross(left, right, **kw):
    return lax.dot_general(
        left, right, (((1,), (1,)), ((), ())), preferred_element_type=F32, **kw
    )


STEPS = 8


def unit_rows_body(block, points_ref, out_ref, held, arrived):
    size = out_ref.shape[0]
    step = size // STEPS
    copies = []
    for at in range(STEPS):
        rows = pl.ds(at * step, step)
        source = points_ref.at[pl.ds(block * size + at * step, step)]
        copies.append(pltpu.make_async_copy(source, held.at[rows], arrived.at[at]))
        copies[-1].start()
    for at in range(STEPS):
        copies[at].wait()
        rows = pl.ds(at * step, step)
        points = held[rows, :]
        mean = jnp.mean(points * points, axis=-1, keepdims=True)
        out_ref[rows, :] = (points * lax.rsqrt(mean + EPSILON)).astype(BF16)


def unit_rows(points, block, size):
    width = points.shape[1]
    return pl.pallas_call(
        functools.partial(unit_rows_body, block),
        in_specs=[pl.BlockSpec(memory_space=pltpu.HBM)],
        out_specs=VMEM,
        out_shape=shaped((size, width), BF16),
        scratch_shapes=[pltpu.VMEM((size, width), F32), pltpu.SemaphoreType.DMA((STEPS,))],
        cost_estimate=pl.CostEstimate(
            flops=3 * size * width, bytes_accessed=6 * size * width, transcendentals=0
        ),
        compiler_params=pltpu.CompilerParams(vmem_limit_bytes=61 << 20),
        name="unit_rows",
    )(points)


def affinity(rows, cols):
    width = rows.shape[1]
    return jnp.exp(cross(rows, cols) * (SHARP / width) - SHARP)


def down(tile):
    return jnp.sum(tile, axis=0, keepdims=True)


def across(tile):
    lanes = 128
    folded = tile[:, :lanes]
    for at in range(lanes, tile.shape[1], lanes):
        folded = folded + tile[:, at : at + lanes]
    return jnp.sum(folded.T, axis=0, keepdims=True)


def gated(mask, sums):
    return jnp.where(mask > 0.0, sums, 0.0)


def span(index, size):
    return slice(index * size, (index + 1) * size)


def x_own(own_mask, l, x, owns, near, first, degree):
    size = x.shape[0]
    for m, cols in enumerate(owns):
        tile = affinity(x[...], cols[...])
        near[span(l - first, size), span(m, size)] = tile.astype(BF16)
        degree[:, span(m, size)] += gated(own_mask[m, l], down(tile))


def own_z(own_mask, owns, m, z, far, degree):
    size = z.shape[0]
    sums = []
    for l, rows in enumerate(owns):
        tile = affinity(rows[...], z[...])
        far[span(l, size), :] = tile.astype(BF16)
        degree[:, span(l, size)] += gated(own_mask[l, 2 * BLK_DEV + m], across(tile))
        sums.append(down(tile))
    return sums


def x_z(x, z, far, at):
    tile = affinity(x[...], z[...])
    far[span(at, z.shape[0]), :] = tile.astype(BF16)
    return down(tile)


def first_tiles_body(own_mask, b0, b1, x0, z0, near, far, degree, far_sums):
    degree[...] = jnp.zeros_like(degree)
    for l, rows in enumerate((b0, b1, x0)):
        x_own(own_mask, l, rows, (b0, b1), near, 0, degree)
    sums = own_z(own_mask, (b0, b1), 0, z0, far, degree)
    sums.append(x_z(x0, z0, far, BLK_DEV))
    for l, line in enumerate(sums):
        far_sums[l : l + 1, :] = line


def last_tiles_body(
    own_mask, far_mask, b0, b1, x0, x1, z0, z1, degree_in, far_sums,
    near, corner, far, degree, far_degree,
):
    size = z0.shape[0]
    degree[...] = degree_in[...]
    x_own(own_mask, BLK_DEV + 1, x1, (b0, b1), near, BLK_DEV + 1, degree)
    early = [far_sums[l : l + 1, :] for l in range(far_sums.shape[0])]
    early.append(x_z(x1, z0, corner, 0))
    late = own_z(own_mask, (b0, b1), 1, z1, far, degree)
    late.append(x_z(x0, z1, far, BLK_DEV))
    late.append(x_z(x1, z1, far, BLK_DEV + 1))
    for m, sums in enumerate((early, late)):
        total = jnp.zeros((1, size), F32)
        for l, line in enumerate(sums):
            total += gated(far_mask[m, l], line)
        far_degree[:, span(m, size)] = total


def kept(mask, m, first, *vectors):
    parts = []
    at = first
    for value in vectors:
        size = value.shape[1] // BLK_DEV
        for l in range(BLK_DEV):
            part = value[:, span(l, size)]
            parts.append(jnp.where(mask[m, at] > 0.0, part, jnp.zeros_like(part)))
            at += 1
    return jnp.concatenate(parts, axis=1)


def apart(left, right):
    return jnp.dot(left, right, preferred_element_type=F32)


def far_rows_body(mask, own, x, far0, corner, far1, out):
    size = own.shape[1] // BLK_DEV
    cut = far0.shape[0]
    left = kept(mask, 0, 0, own, x)
    out[:, span(0, size)] = apart(left[:, :cut], far0[...]) + apart(left[:, cut:], corner[...])
    out[:, span(1, size)] = apart(kept(mask, 1, 0, own, x), far1[...])


def near_rows_body(mask, own, x, z, near0, near1, far0, far1, out):
    size = own.shape[1] // BLK_DEV
    cut = near0.shape[0]
    for m in range(BLK_DEV):
        there = span(m, size)
        left = kept(mask, m, 0, own, x)
        side = kept(mask, m, 2 * BLK_DEV, z)
        total = apart(left[:, :cut], near0[:, there]) + apart(left[:, cut:], near1[:, there])
        total += cross(side[:, :size], far0[there, :]) + cross(side[:, size:], far1[there, :])
        out[:, there] = total


def join_body(near, given, root, image, ahead, gram):
    full = (near[...] + given[...]) * root[...]
    image[...] = full
    ahead[...] = full * root[...]
    gram[...] = cross(full, full, precision=EXACT)


GROUP = 8


def inverse_factor(gram):
    size = gram.shape[0]
    rows = lax.broadcasted_iota(jnp.int32, (size, 2 * size), 0)
    lanes = lax.broadcasted_iota(jnp.int32, (size, 2 * size), 1)
    unit = jnp.where(rows + size == lanes, 1.0, 0.0).astype(F32)
    live = jnp.concatenate([gram, unit[:, size:]], axis=1)
    finished = []
    for first in range(0, size, GROUP):
        cols = [
            jnp.broadcast_to(live[:, first + b : first + b + 1], live.shape) for b in range(GROUP)
        ]
        lines = [live[a : a + 1, :] for a in range(GROUP)]
        pivots = {(a, b): cols[b][a : a + 1, :] for a in range(GROUP) for b in range(a, GROUP)}
        change = jnp.zeros_like(live)
        for a in range(GROUP):
            inverse = 1.0 / pivots[a, a]
            for b in range(a + 1, GROUP):
                ratio = pivots[a, b] * inverse
                lines[b] = lines[b] - ratio * lines[a]
                cols[b] = cols[b] - ratio * cols[a]
                for c in range(b, GROUP):
                    pivots[b, c] = pivots[b, c] - ratio * pivots[a, c]
            change += cols[a] * inverse * lines[a]
            finished.append(lines[a] * lax.rsqrt(pivots[a, a]))
        if first + GROUP < size:
            live = (live - change)[GROUP:, :]
    return jnp.concatenate(finished, axis=0)[:, size:]


def solve_body(scale, gram, *refs):
    factor = inverse_factor(gram[...]) * scale
    count = len(refs) // 2
    for value, out in zip(refs[:count], refs[count:]):
        solved = jnp.dot(factor, value[...], preferred_element_type=F32, precision=EXACT)
        out[...] = solved.astype(out.dtype)


def exchange_masks(row_count, col_count):
    low = [1 << bit for bit in range(col_count.bit_length() - 1)]
    high = [col_count << bit for bit in range(row_count.bit_length() - 1)]
    stages = [(high[0], low[0]), (high[1],), (low[1], low[2])]
    rest = high[2:] + low[3:]
    return stages + [tuple(rest[at : at + 2]) for at in range(0, len(rest), 2)]


def total_sum(value):
    row_count = lax.axis_size("row")
    col_count = lax.axis_size("col")
    devices = row_count * col_count
    if devices & (devices - 1) or row_count < 4 or col_count < 8:
        return lax.psum(value, ("row", "col"))

    def fetched(mask):
        pairs = [(source, source ^ mask) for source in range(devices)]
        return lax.ppermute(value, ("row", "col"), pairs)

    for masks in exchange_masks(row_count, col_count):
        if len(masks) == 1:
            value = value + fetched(masks[0])
        else:
            first, second = masks
            near, far, both = fetched(first), fetched(second), fetched(first ^ second)
            value = (value + near) + (far + both)
    return value


def listed(ids, blocks):
    found = jnp.zeros((ids.shape[0], blocks.shape[0]), bool)
    for slot in range(ids.shape[1]):
        found = found | (ids[:, slot : slot + 1] == blocks[None, :])
    return found.astype(F32)


def on_device(embeddings, neighbour_ids, start_vectors):
    col_count = lax.axis_size("col")
    col = lax.axis_index("col")
    base = lax.axis_index("row") * col_count
    points, width = embeddings.shape
    columns = start_vectors.shape[1]
    size = points // BLK_DEV
    total_rows = points * lax.axis_size("row") * col_count

    def side_of(index):
        return (index + (REACH if index % 2 == 0 else -REACH)) % col_count

    def from_x(value):
        return lax.ppermute(value, "col", [(i, i ^ 1) for i in range(col_count)])

    def from_z(value):
        return lax.ppermute(value, "col", [(side_of(i), i) for i in range(col_count)])

    def to_z(value):
        return lax.ppermute(value, "col", [(i, side_of(i)) for i in range(col_count)])

    b0 = unit_rows(embeddings, 0, size)
    z0 = from_z(b0)
    x0 = from_x(b0)
    b1 = unit_rows(embeddings, 1, size)
    z1 = from_z(b1)
    x1 = from_x(b1)
    far_ids = from_z(neighbour_ids)

    here = base + col
    x_side = base + (col ^ 1)
    z_side = base + (col + jnp.where(col % 2 == 0, REACH, col_count - REACH)) % col_count
    members = jnp.arange(BLK_DEV, dtype=jnp.int32)
    nearby = jnp.stack([here, x_side, z_side])[:, None] * BLK_DEV + members[None, :]
    nearby = nearby.reshape(-1)
    own_mask = listed(neighbour_ids, nearby)
    far_mask = listed(far_ids, nearby[: 2 * BLK_DEV])

    line = shaped((1, points), F32)
    one = 2 * size * size * width
    moved = 4 * size * width
    most = 2 * BLK_DEV - 1
    near0, far0, degree, far_sums = call(
        first_tiles_body,
        (
            shaped((most * size, points), BF16), shaped((most * size, size), BF16), line,
            shaped((most, size), F32),
        ),
        [SMEM] + [VMEM] * 4, 9 * one, 9 * moved,
    )(own_mask, b0, b1, x0, z0)
    near1, corner, far1, degree, far_degree = call(
        last_tiles_body,
        (
            shaped((size, points), BF16), shaped((size, size), BF16),
            shaped((2 * points, size), BF16), line, line,
        ),
        [SMEM] * 2 + [VMEM] * 8, 7 * one, 7 * moved,
    )(own_mask, far_mask, b0, b1, x0, x1, z0, z1, degree, far_sums)
    root = lax.rsqrt(degree + to_z(far_degree))

    across_shape = (columns, points)
    work = 2 * columns * size * size
    wide = shaped(across_shape, F32)
    far_rows = call(far_rows_body, wide, [SMEM] + [VMEM] * 5, 8 * work, 8 * work // 64)
    near_rows = call(near_rows_body, wide, [SMEM] + [VMEM] * 7, 12 * work, 12 * work // 64)
    join = call(
        join_body,
        (wide, wide, shaped((columns, columns), F32)),
        [VMEM] * 3, 2 * columns * columns * points, 4 * columns * points,
    )

    def solve(dtype, gram, *values):
        return call(
            functools.partial(solve_body, math.sqrt(total_rows)),
            tuple(shaped(across_shape, dtype) for _ in values),
            [VMEM] * (1 + len(values)),
            4 * columns * columns * points, 4 * columns * points,
        )(gram, *values)

    own = (start_vectors.T * root).astype(BF16)
    x = from_x(own)
    z = from_z(own)
    for iteration in range(ITERS):
        sent = far_rows(far_mask, own, x, far0, corner, far1)
        given = to_z(sent)
        held = near_rows(own_mask, own, x, z, near0, near1, far0, far1)
        image, ahead, gram = join(held, given, root)
        if iteration < ITERS - 1:
            ahead_x, ahead_z = from_x(ahead), from_z(ahead)
            total = total_sum(gram)
            own, x, z = solve(BF16, total, ahead, ahead_x, ahead_z)
    (vectors,) = solve(F32, total_sum(gram), image)
    return vectors.T


def solution(mesh):
    in_specs = (P(("row", "col"), None), P(("row", "col"), None), P(("row", "col"), None))
    out_specs = P(("row", "col"), None)
    return jax.shard_map(on_device, mesh=mesh, in_specs=in_specs, out_specs=out_specs, check_vma=False)
```

```python
import functools
import math

import jax
import jax.numpy as jnp
from jax import lax
from jax.experimental import pallas as pl
from jax.experimental.pallas import tpu as pltpu
from jax.sharding import PartitionSpec as P

REACH = 2
ITERS = 3
BLK_DEV = 2

SHARP = 8.0
EPSILON = 1e-06

F32 = jnp.float32
BF16 = jnp.bfloat16
EXACT = lax.Precision.HIGHEST
VMEM = pl.BlockSpec(memory_space=pltpu.VMEM)
SMEM = pl.BlockSpec(memory_space=pltpu.SMEM)


def call(body, out_shape, in_specs, flops, moved, room=6, aliases=None):
    return pl.pallas_call(
        body,
        out_shape=out_shape,
        in_specs=in_specs,
        out_specs=jax.tree.map(lambda _: VMEM, out_shape),
        input_output_aliases=aliases or {},
        cost_estimate=pl.CostEstimate(flops=flops, bytes_accessed=moved, transcendentals=0),
        compiler_params=pltpu.CompilerParams(vmem_limit_bytes=room << 20),
    )


def shaped(shape, dtype):
    return jax.ShapeDtypeStruct(shape, dtype)


def cross(left, right, **kw):
    return lax.dot_general(
        left, right, (((1,), (1,)), ((), ())), preferred_element_type=F32, **kw
    )


STEPS = 8


def unit_rows_body(block, points_ref, out_ref, held, arrived):
    size = out_ref.shape[0]
    step = size // STEPS
    copies = []
    for at in range(STEPS):
        rows = pl.ds(at * step, step)
        source = points_ref.at[pl.ds(block * size + at * step, step)]
        copies.append(pltpu.make_async_copy(source, held.at[rows], arrived.at[at]))
        copies[-1].start()
    for at in range(STEPS):
        copies[at].wait()
        rows = pl.ds(at * step, step)
        points = held[rows, :]
        mean = jnp.mean(points * points, axis=-1, keepdims=True)
        out_ref[rows, :] = (points * lax.rsqrt(mean + EPSILON)).astype(BF16)


def unit_rows(points, block, size):
    width = points.shape[1]
    return pl.pallas_call(
        functools.partial(unit_rows_body, block),
        in_specs=[pl.BlockSpec(memory_space=pltpu.HBM)],
        out_specs=VMEM,
        out_shape=shaped((size, width), BF16),
        scratch_shapes=[pltpu.VMEM((size, width), F32), pltpu.SemaphoreType.DMA((STEPS,))],
        cost_estimate=pl.CostEstimate(
            flops=3 * size * width, bytes_accessed=6 * size * width, transcendentals=0
        ),
        compiler_params=pltpu.CompilerParams(vmem_limit_bytes=61 << 20),
        name="unit_rows",
    )(points)


def affinity(rows, cols):
    width = rows.shape[1]
    return jnp.exp(cross(rows, cols) * (SHARP / width) - SHARP)


def down(tile):
    return jnp.sum(tile, axis=0, keepdims=True)


def across(tile):
    lanes = 128
    folded = tile[:, :lanes]
    for at in range(lanes, tile.shape[1], lanes):
        folded = folded + tile[:, at : at + lanes]
    return jnp.sum(folded.T, axis=0, keepdims=True)


def gated(mask, sums):
    return jnp.where(mask > 0.0, sums, 0.0)


def span(index, size):
    return slice(index * size, (index + 1) * size)


def x_own(own_mask, l, x, owns, near, first, degree):
    size = x.shape[0]
    for m, cols in enumerate(owns):
        tile = affinity(x[...], cols[...])
        near[span(l - first, size), span(m, size)] = tile.astype(BF16)
        degree[:, span(m, size)] += gated(own_mask[m, l], down(tile))


def own_z(own_mask, owns, m, z, far, degree):
    size = z.shape[0]
    sums = []
    for l, rows in enumerate(owns):
        tile = affinity(rows[...], z[...])
        far[span(l, size), :] = tile.astype(BF16)
        degree[:, span(l, size)] += gated(own_mask[l, 2 * BLK_DEV + m], across(tile))
        sums.append(down(tile))
    return sums


def x_z(x, z, far, at):
    tile = affinity(x[...], z[...])
    far[span(at, z.shape[0]), :] = tile.astype(BF16)
    return down(tile)


def first_tiles_body(own_mask, b0, b1, x0, z0, near, far, degree, far_sums):
    degree[...] = jnp.zeros_like(degree)
    for l, rows in enumerate((b0, b1, x0)):
        x_own(own_mask, l, rows, (b0, b1), near, 0, degree)
    sums = own_z(own_mask, (b0, b1), 0, z0, far, degree)
    sums.append(x_z(x0, z0, far, BLK_DEV))
    for l, line in enumerate(sums):
        far_sums[l : l + 1, :] = line


def last_tiles_body(
    own_mask, far_mask, b0, b1, x0, x1, z0, z1, degree_in, far_sums,
    near, corner, far, degree, far_degree,
):
    size = z0.shape[0]
    degree[...] = degree_in[...]
    x_own(own_mask, BLK_DEV + 1, x1, (b0, b1), near, BLK_DEV + 1, degree)
    early = [far_sums[l : l + 1, :] for l in range(far_sums.shape[0])]
    early.append(x_z(x1, z0, corner, 0))
    late = own_z(own_mask, (b0, b1), 1, z1, far, degree)
    late.append(x_z(x0, z1, far, BLK_DEV))
    late.append(x_z(x1, z1, far, BLK_DEV + 1))
    for m, sums in enumerate((early, late)):
        total = jnp.zeros((1, size), F32)
        for l, line in enumerate(sums):
            total += gated(far_mask[m, l], line)
        far_degree[:, span(m, size)] = total


def bfloat_rows(value):
    if value.dtype == BF16:
        return value
    high = value.astype(BF16)
    rest = value - high.astype(F32)
    middle = rest.astype(BF16)
    low = (rest - middle.astype(F32)).astype(BF16)
    return jnp.concatenate([high, middle, low], axis=0)


def whole_rows(value, count):
    if value.shape[0] == count:
        return value
    return (value[2 * count :] + value[count : 2 * count]) + value[:count]


def kept(mask, m, first, *vectors):
    parts = []
    at = first
    for value in vectors:
        size = value.shape[1] // BLK_DEV
        for l in range(BLK_DEV):
            part = value[:, span(l, size)]
            parts.append(jnp.where(mask[m, at] > 0.0, part, jnp.zeros_like(part)))
            at += 1
    return jnp.concatenate(parts, axis=1)


def apart(left, right):
    return jnp.dot(left, right, preferred_element_type=F32)


def far_rows_body(mask, own_ref, x_ref, far0, corner, far1, out):
    own, x = bfloat_rows(own_ref[...]), bfloat_rows(x_ref[...])
    size = own.shape[1] // BLK_DEV
    count = out.shape[0]
    cut = far0.shape[0]
    left = kept(mask, 0, 0, own, x)
    first = apart(left[:, :cut], far0[...]) + apart(left[:, cut:], corner[...])
    out[:, span(0, size)] = whole_rows(first, count)
    out[:, span(1, size)] = whole_rows(apart(kept(mask, 1, 0, own, x), far1[...]), count)


def near_rows_body(mask, own_ref, x_ref, z_ref, near0, near1, far0, far1, out):
    own, x, z = bfloat_rows(own_ref[...]), bfloat_rows(x_ref[...]), bfloat_rows(z_ref[...])
    size = own.shape[1] // BLK_DEV
    cut = near0.shape[0]
    for m in range(BLK_DEV):
        there = span(m, size)
        left = kept(mask, m, 0, own, x)
        side = kept(mask, m, 2 * BLK_DEV, z)
        total = apart(left[:, :cut], near0[:, there]) + apart(left[:, cut:], near1[:, there])
        total += cross(side[:, :size], far0[there, :]) + cross(side[:, size:], far1[there, :])
        out[:, there] = whole_rows(total, out.shape[0])


def finish(full, root, image, ahead, gram):
    image[...] = full
    ahead[...] = full * root[...]
    gram[...] = cross(full, full, precision=EXACT)


def join_body(near, given, root, image, ahead, gram):
    finish((near[...] + given[...]) * root[...], root, image, ahead, gram)


def advance_body(scale, total, near, given, root, image, ahead, gram):
    factor = inverse_factor(total[...]) * scale
    full = (near[...] + given[...]) * root[...]
    solved = jnp.dot(factor, full, preferred_element_type=F32, precision=EXACT)
    finish(solved, root, image, ahead, gram)


GROUP = 8


def inverse_factor(gram):
    size = gram.shape[0]
    rows = lax.broadcasted_iota(jnp.int32, (size, 2 * size), 0)
    lanes = lax.broadcasted_iota(jnp.int32, (size, 2 * size), 1)
    unit = jnp.where(rows + size == lanes, 1.0, 0.0).astype(F32)
    live = jnp.concatenate([gram, unit[:, size:]], axis=1)
    finished = []
    for first in range(0, size, GROUP):
        cols = [
            jnp.broadcast_to(live[:, first + b : first + b + 1], live.shape) for b in range(GROUP)
        ]
        lines = [live[a : a + 1, :] for a in range(GROUP)]
        pivots = {(a, b): cols[b][a : a + 1, :] for a in range(GROUP) for b in range(a, GROUP)}
        change = jnp.zeros_like(live)
        for a in range(GROUP):
            inverse = 1.0 / pivots[a, a]
            for b in range(a + 1, GROUP):
                ratio = pivots[a, b] * inverse
                lines[b] = lines[b] - ratio * lines[a]
                cols[b] = cols[b] - ratio * cols[a]
                for c in range(b, GROUP):
                    pivots[b, c] = pivots[b, c] - ratio * pivots[a, c]
            change += cols[a] * inverse * lines[a]
            finished.append(lines[a] * lax.rsqrt(pivots[a, a]))
        if first + GROUP < size:
            live = (live - change)[GROUP:, :]
    return jnp.concatenate(finished, axis=0)[:, size:]


def solve_body(scale, total, image, out):
    factor = inverse_factor(total[...]) * scale
    out[...] = jnp.dot(factor, image[...], preferred_element_type=F32, precision=EXACT)


def exchange_masks(row_count, col_count):
    low = [1 << bit for bit in range(col_count.bit_length() - 1)]
    high = [col_count << bit for bit in range(row_count.bit_length() - 1)]
    stages = [(low[1], low[2]), (high[0], high[1]), (low[0],)]
    rest = high[2:] + low[3:]
    return stages + [tuple(rest[at : at + 2]) for at in range(0, len(rest), 2)]


def total_sum(value):
    row_count = lax.axis_size("row")
    col_count = lax.axis_size("col")
    devices = row_count * col_count
    if devices & (devices - 1) or row_count < 4 or col_count < 8:
        return lax.psum(value, ("row", "col"))

    def fetched(mask):
        pairs = [(source, source ^ mask) for source in range(devices)]
        return lax.ppermute(value, ("row", "col"), pairs)

    for masks in exchange_masks(row_count, col_count):
        if len(masks) == 1:
            value = value + fetched(masks[0])
        else:
            first, second = masks
            near, far, both = fetched(first), fetched(second), fetched(first ^ second)
            value = (value + near) + (far + both)
    return value


def listed(ids, blocks):
    found = jnp.zeros((ids.shape[0], blocks.shape[0]), bool)
    for slot in range(ids.shape[1]):
        found = found | (ids[:, slot : slot + 1] == blocks[None, :])
    return found.astype(F32)


def on_device(embeddings, neighbour_ids, start_vectors):
    col_count = lax.axis_size("col")
    col = lax.axis_index("col")
    base = lax.axis_index("row") * col_count
    points, width = embeddings.shape
    columns = start_vectors.shape[1]
    size = points // BLK_DEV
    total_rows = points * lax.axis_size("row") * col_count

    def side_of(index):
        return (index + (REACH if index % 2 == 0 else -REACH)) % col_count

    def from_x(value):
        return lax.ppermute(value, "col", [(i, i ^ 1) for i in range(col_count)])

    def from_z(value):
        return lax.ppermute(value, "col", [(side_of(i), i) for i in range(col_count)])

    def to_z(value):
        return lax.ppermute(value, "col", [(i, side_of(i)) for i in range(col_count)])

    b0 = unit_rows(embeddings, 0, size)
    z0 = from_z(b0)
    x0 = from_x(b0)
    b1 = unit_rows(embeddings, 1, size)
    z1 = from_z(b1)
    x1 = from_x(b1)
    far_ids = from_z(neighbour_ids)

    here = base + col
    x_side = base + (col ^ 1)
    z_side = base + (col + jnp.where(col % 2 == 0, REACH, col_count - REACH)) % col_count
    members = jnp.arange(BLK_DEV, dtype=jnp.int32)
    nearby = jnp.stack([here, x_side, z_side])[:, None] * BLK_DEV + members[None, :]
    nearby = nearby.reshape(-1)
    own_mask = listed(neighbour_ids, nearby)
    far_mask = listed(far_ids, nearby[: 2 * BLK_DEV])

    line = shaped((1, points), F32)
    one = 2 * size * size * width
    moved = 4 * size * width
    most = 2 * BLK_DEV - 1
    near0, far0, degree, far_sums = call(
        first_tiles_body,
        (
            shaped((most * size, points), BF16), shaped((most * size, size), BF16), line,
            shaped((most, size), F32),
        ),
        [SMEM] + [VMEM] * 4, 9 * one, 9 * moved,
    )(own_mask, b0, b1, x0, z0)
    near1, corner, far1, degree, far_degree = call(
        last_tiles_body,
        (
            shaped((size, points), BF16), shaped((size, size), BF16),
            shaped((2 * points, size), BF16), line, line,
        ),
        [SMEM] * 2 + [VMEM] * 8, 7 * one, 7 * moved,
    )(own_mask, far_mask, b0, b1, x0, x1, z0, z1, degree, far_sums)
    root = lax.rsqrt(degree + to_z(far_degree))

    across_shape = (columns, points)
    work = 2 * columns * size * size
    wide = shaped(across_shape, F32)
    far_rows = call(far_rows_body, wide, [SMEM] + [VMEM] * 5, 8 * work, 8 * work // 64)
    near_rows = call(near_rows_body, wide, [SMEM] + [VMEM] * 7, 12 * work, 12 * work // 64)
    results = (wide, wide, shaped((columns, columns), F32))
    effort = 2 * columns * columns * points, 4 * columns * points
    scale = math.sqrt(total_rows)
    join = call(join_body, results, [VMEM] * 3, *effort)
    advance = call(functools.partial(advance_body, scale), results, [VMEM] * 4, *effort)
    solve = call(functools.partial(solve_body, scale), wide, [VMEM] * 2, *effort)

    own = (start_vectors.T * root).astype(BF16)
    for step in range(ITERS):
        x = from_x(own)
        z = from_z(own)
        sent = far_rows(far_mask, own, x, far0, corner, far1)
        given = to_z(sent)
        held = near_rows(own_mask, own, x, z, near0, near1, far0, far1)
        if step == 0:
            image, own, gram = join(held, given, root)
        else:
            image, own, gram = advance(total, held, given, root)
        total = total_sum(gram)
    return solve(total, image).T


def solution(mesh):
    in_specs = (P(("row", "col"), None), P(("row", "col"), None), P(("row", "col"), None))
    out_specs = P(("row", "col"), None)
    return jax.shard_map(on_device, mesh=mesh, in_specs=in_specs, out_specs=out_specs, check_vma=False)
```

```python
import functools
import math

import jax
import jax.numpy as jnp
from jax import lax
from jax.experimental import pallas as pl
from jax.experimental.pallas import tpu as pltpu
from jax.sharding import PartitionSpec as P

REACH = 2
ITERS = 3
BLK_DEV = 2

SHARP = 8.0
EPSILON = 1e-06

F32 = jnp.float32
BF16 = jnp.bfloat16
EXACT = lax.Precision.HIGHEST
VMEM = pl.BlockSpec(memory_space=pltpu.VMEM)
SMEM = pl.BlockSpec(memory_space=pltpu.SMEM)


def call(body, out_shape, in_specs, flops, moved, room=6, aliases=None):
    return pl.pallas_call(
        body,
        out_shape=out_shape,
        in_specs=in_specs,
        out_specs=jax.tree.map(lambda _: VMEM, out_shape),
        input_output_aliases=aliases or {},
        cost_estimate=pl.CostEstimate(flops=flops, bytes_accessed=moved, transcendentals=0),
        compiler_params=pltpu.CompilerParams(vmem_limit_bytes=room << 20),
    )


def shaped(shape, dtype):
    return jax.ShapeDtypeStruct(shape, dtype)


def cross(left, right, **kw):
    return lax.dot_general(
        left, right, (((1,), (1,)), ((), ())), preferred_element_type=F32, **kw
    )


STEPS = 8


def unit_rows_body(block, points_ref, out_ref, held, arrived):
    size = out_ref.shape[0]
    step = size // STEPS
    copies = []
    for at in range(STEPS):
        rows = pl.ds(at * step, step)
        source = points_ref.at[pl.ds(block * size + at * step, step)]
        copies.append(pltpu.make_async_copy(source, held.at[rows], arrived.at[at]))
        copies[-1].start()
    for at in range(STEPS):
        copies[at].wait()
        rows = pl.ds(at * step, step)
        points = held[rows, :]
        mean = jnp.mean(points * points, axis=-1, keepdims=True)
        out_ref[rows, :] = (points * lax.rsqrt(mean + EPSILON)).astype(BF16)


def unit_rows(points, block, size):
    width = points.shape[1]
    return pl.pallas_call(
        functools.partial(unit_rows_body, block),
        in_specs=[pl.BlockSpec(memory_space=pltpu.HBM)],
        out_specs=VMEM,
        out_shape=shaped((size, width), BF16),
        scratch_shapes=[pltpu.VMEM((size, width), F32), pltpu.SemaphoreType.DMA((STEPS,))],
        cost_estimate=pl.CostEstimate(
            flops=3 * size * width, bytes_accessed=6 * size * width, transcendentals=0
        ),
        compiler_params=pltpu.CompilerParams(vmem_limit_bytes=4 << 20),
        name="unit_rows",
    )(pltpu.with_memory_space_constraint(points, pltpu.HBM))


def affinity(rows, cols):
    width = rows.shape[1]
    return jnp.exp(cross(rows, cols) * (SHARP / width) - SHARP)


def down(tile):
    return jnp.sum(tile, axis=0, keepdims=True)


def across(tile):
    lanes = 128
    folded = tile[:, :lanes]
    for at in range(lanes, tile.shape[1], lanes):
        folded = folded + tile[:, at : at + lanes]
    return jnp.sum(folded.T, axis=0, keepdims=True)


def gated(mask, sums):
    return jnp.where(mask > 0.0, sums, 0.0)


def span(index, size):
    return slice(index * size, (index + 1) * size)


def x_own(own_mask, l, x, owns, near, first, degree):
    size = x.shape[0]
    for m, cols in enumerate(owns):
        tile = affinity(x[...], cols[...])
        near[span(l - first, size), span(m, size)] = tile.astype(BF16)
        degree[:, span(m, size)] += gated(own_mask[m, l], down(tile))


def own_z(own_mask, owns, m, z, far, degree):
    size = z.shape[0]
    sums = []
    for l, rows in enumerate(owns):
        tile = affinity(rows[...], z[...])
        far[span(l, size), :] = tile.astype(BF16)
        degree[:, span(l, size)] += gated(own_mask[l, 2 * BLK_DEV + m], across(tile))
        sums.append(down(tile))
    return sums


def x_z(x, z, far, at):
    tile = affinity(x[...], z[...])
    far[span(at, z.shape[0]), :] = tile.astype(BF16)
    return down(tile)


def first_tiles_body(own_mask, b0, b1, x0, z0, near, far, degree, far_sums):
    degree[...] = jnp.zeros_like(degree)
    for l, rows in enumerate((b0, b1, x0)):
        x_own(own_mask, l, rows, (b0, b1), near, 0, degree)
    sums = own_z(own_mask, (b0, b1), 0, z0, far, degree)
    sums.append(x_z(x0, z0, far, BLK_DEV))
    for l, line in enumerate(sums):
        far_sums[l : l + 1, :] = line


def last_tiles_body(
    own_mask, far_mask, b0, b1, x0, x1, z0, z1, degree_in, far_sums,
    near, corner, far, degree, far_degree,
):
    size = z0.shape[0]
    degree[...] = degree_in[...]
    x_own(own_mask, BLK_DEV + 1, x1, (b0, b1), near, BLK_DEV + 1, degree)
    early = [far_sums[l : l + 1, :] for l in range(far_sums.shape[0])]
    early.append(x_z(x1, z0, corner, 0))
    late = own_z(own_mask, (b0, b1), 1, z1, far, degree)
    late.append(x_z(x0, z1, far, BLK_DEV))
    late.append(x_z(x1, z1, far, BLK_DEV + 1))
    for m, sums in enumerate((early, late)):
        total = jnp.zeros((1, size), F32)
        for l, line in enumerate(sums):
            total += gated(far_mask[m, l], line)
        far_degree[:, span(m, size)] = total


def bfloat_rows(value):
    if value.dtype == BF16:
        return value
    high = value.astype(BF16)
    rest = value - high.astype(F32)
    middle = rest.astype(BF16)
    low = (rest - middle.astype(F32)).astype(BF16)
    return jnp.concatenate([high, middle, low], axis=0)


def whole_rows(value, count):
    if value.shape[0] == count:
        return value
    return (value[2 * count :] + value[count : 2 * count]) + value[:count]


def kept(mask, m, first, *vectors):
    parts = []
    at = first
    for value in vectors:
        size = value.shape[1] // BLK_DEV
        for l in range(BLK_DEV):
            part = value[:, span(l, size)]
            parts.append(jnp.where(mask[m, at] > 0.0, part, jnp.zeros_like(part)))
            at += 1
    return jnp.concatenate(parts, axis=1)


def apart(left, right):
    return jnp.dot(left, right, preferred_element_type=F32)


def far_rows_body(mask, own_ref, x_ref, far0, corner, far1, out):
    own, x = bfloat_rows(own_ref[...]), bfloat_rows(x_ref[...])
    size = own.shape[1] // BLK_DEV
    count = out.shape[0]
    cut = far0.shape[0]
    left = kept(mask, 0, 0, own, x)
    first = apart(left[:, :cut], far0[...]) + apart(left[:, cut:], corner[...])
    out[:, span(0, size)] = whole_rows(first, count)
    out[:, span(1, size)] = whole_rows(apart(kept(mask, 1, 0, own, x), far1[...]), count)


def near_rows_body(mask, own_ref, x_ref, z_ref, near0, near1, far0, far1, out):
    own, x, z = bfloat_rows(own_ref[...]), bfloat_rows(x_ref[...]), bfloat_rows(z_ref[...])
    size = own.shape[1] // BLK_DEV
    cut = near0.shape[0]
    for m in range(BLK_DEV):
        there = span(m, size)
        left = kept(mask, m, 0, own, x)
        side = kept(mask, m, 2 * BLK_DEV, z)
        total = apart(left[:, :cut], near0[:, there]) + apart(left[:, cut:], near1[:, there])
        total += cross(side[:, :size], far0[there, :]) + cross(side[:, size:], far1[there, :])
        out[:, there] = whole_rows(total, out.shape[0])


def finish(full, root, image, ahead, gram):
    image[...] = full
    ahead[...] = full * root[...]
    gram[...] = cross(full, full, precision=EXACT)


def join_body(near, given, root, image, ahead, gram):
    finish((near[...] + given[...]) * root[...], root, image, ahead, gram)


def advance_body(scale, total, near, given, root, image, ahead, gram):
    factor = inverse_factor(total[...]) * scale
    full = (near[...] + given[...]) * root[...]
    solved = jnp.dot(factor, full, preferred_element_type=F32, precision=EXACT)
    finish(solved, root, image, ahead, gram)


GROUP = 8


def inverse_factor(gram):
    size = gram.shape[0]
    rows = lax.broadcasted_iota(jnp.int32, (size, 2 * size), 0)
    lanes = lax.broadcasted_iota(jnp.int32, (size, 2 * size), 1)
    unit = jnp.where(rows + size == lanes, 1.0, 0.0).astype(F32)
    live = jnp.concatenate([gram, unit[:, size:]], axis=1)
    finished = []
    for first in range(0, size, GROUP):
        cols = [
            jnp.broadcast_to(live[:, first + b : first + b + 1], live.shape) for b in range(GROUP)
        ]
        lines = [live[a : a + 1, :] for a in range(GROUP)]
        pivots = {(a, b): cols[b][a : a + 1, :] for a in range(GROUP) for b in range(a, GROUP)}
        change = jnp.zeros_like(live)
        for a in range(GROUP):
            inverse = 1.0 / pivots[a, a]
            for b in range(a + 1, GROUP):
                ratio = pivots[a, b] * inverse
                lines[b] = lines[b] - ratio * lines[a]
                cols[b] = cols[b] - ratio * cols[a]
                for c in range(b, GROUP):
                    pivots[b, c] = pivots[b, c] - ratio * pivots[a, c]
            change += cols[a] * inverse * lines[a]
            finished.append(lines[a] * lax.rsqrt(pivots[a, a]))
        if first + GROUP < size:
            live = (live - change)[GROUP:, :]
    return jnp.concatenate(finished, axis=0)[:, size:]


def solve_body(scale, total, image, out):
    factor = inverse_factor(total[...]) * scale
    out[...] = jnp.dot(factor, image[...], preferred_element_type=F32, precision=EXACT)


def exchange_masks(row_count, col_count, alone):
    low = [1 << bit for bit in range(col_count.bit_length() - 1)]
    high = [col_count << bit for bit in range(row_count.bit_length() - 1)]
    if alone:
        stages = [(high[0],), (high[1], low[0]), (low[1], low[2])]
    else:
        stages = [(low[1], low[2]), (high[0], high[1]), (low[0],)]
    rest = high[2:] + low[3:]
    return stages + [tuple(rest[at : at + 2]) for at in range(0, len(rest), 2)]


def total_sum(value, alone):
    row_count = lax.axis_size("row")
    col_count = lax.axis_size("col")
    devices = row_count * col_count
    if devices & (devices - 1) or row_count < 4 or col_count < 8:
        return lax.psum(value, ("row", "col"))

    def fetched(mask):
        pairs = [(source, source ^ mask) for source in range(devices)]
        return lax.ppermute(value, ("row", "col"), pairs)

    for masks in exchange_masks(row_count, col_count, alone):
        if len(masks) == 1:
            value = value + fetched(masks[0])
        else:
            first, second = masks
            near, far, both = fetched(first), fetched(second), fetched(first ^ second)
            value = (value + near) + (far + both)
    return value


def listed(ids, blocks):
    found = jnp.zeros((ids.shape[0], blocks.shape[0]), bool)
    for slot in range(ids.shape[1]):
        found = found | (ids[:, slot : slot + 1] == blocks[None, :])
    return found.astype(F32)


def on_device(embeddings, neighbour_ids, start_vectors):
    col_count = lax.axis_size("col")
    col = lax.axis_index("col")
    base = lax.axis_index("row") * col_count
    points, width = embeddings.shape
    columns = start_vectors.shape[1]
    size = points // BLK_DEV
    total_rows = points * lax.axis_size("row") * col_count

    def side_of(index):
        return (index + (REACH if index % 2 == 0 else -REACH)) % col_count

    def from_x(value):
        return lax.ppermute(value, "col", [(i, i ^ 1) for i in range(col_count)])

    def from_z(value):
        return lax.ppermute(value, "col", [(side_of(i), i) for i in range(col_count)])

    def to_z(value):
        return lax.ppermute(value, "col", [(i, side_of(i)) for i in range(col_count)])

    def to_z_side(value):
        return lax.ppermute(value, "col", [(i, side_of(i) ^ 1) for i in range(col_count)])

    b0 = unit_rows(embeddings, 0, size)
    z0 = from_z(b0)
    x0 = from_x(b0)
    b1 = unit_rows(embeddings, 1, size)
    z1 = from_z(b1)
    x1 = from_x(b1)
    far_ids = from_z(neighbour_ids)
    start = start_vectors.T
    start_x = from_x(start)
    start_z = from_z(start)

    here = base + col
    x_side = base + (col ^ 1)
    z_side = base + (col + jnp.where(col % 2 == 0, REACH, col_count - REACH)) % col_count
    members = jnp.arange(BLK_DEV, dtype=jnp.int32)
    nearby = jnp.stack([here, x_side, z_side])[:, None] * BLK_DEV + members[None, :]
    nearby = nearby.reshape(-1)
    own_mask = listed(neighbour_ids, nearby)
    far_mask = listed(far_ids, nearby[: 2 * BLK_DEV])

    line = shaped((1, points), F32)
    one = 2 * size * size * width
    moved = 4 * size * width
    most = 2 * BLK_DEV - 1
    near0, far0, degree, far_sums = call(
        first_tiles_body,
        (
            shaped((most * size, points), BF16), shaped((most * size, size), BF16), line,
            shaped((most, size), F32),
        ),
        [SMEM] + [VMEM] * 4, 9 * one, 9 * moved,
    )(own_mask, b0, b1, x0, z0)
    near1, corner, far1, degree, far_degree = call(
        last_tiles_body,
        (
            shaped((size, points), BF16), shaped((size, size), BF16),
            shaped((2 * points, size), BF16), line, line,
        ),
        [SMEM] * 2 + [VMEM] * 8, 7 * one, 7 * moved,
    )(own_mask, far_mask, b0, b1, x0, x1, z0, z1, degree, far_sums)
    root = lax.rsqrt(degree + to_z(far_degree))
    root_x = lax.rsqrt(from_x(degree) + to_z_side(far_degree))
    root_z = lax.rsqrt(from_z(degree) + far_degree)

    across_shape = (columns, points)
    work = 2 * columns * size * size
    wide = shaped(across_shape, F32)
    far_rows = call(far_rows_body, wide, [SMEM] + [VMEM] * 5, 8 * work, 8 * work // 64)
    near_rows = call(near_rows_body, wide, [SMEM] + [VMEM] * 7, 12 * work, 12 * work // 64)
    results = (wide, wide, shaped((columns, columns), F32))
    effort = 2 * columns * columns * points, 4 * columns * points
    scale = math.sqrt(total_rows)
    join = call(join_body, results, [VMEM] * 3, *effort)
    advance = call(functools.partial(advance_body, scale), results, [VMEM] * 4, *effort)
    solve = call(functools.partial(solve_body, scale), wide, [VMEM] * 2, *effort)

    own, x, z = (
        (value * line).astype(BF16)
        for value, line in ((start, root), (start_x, root_x), (start_z, root_z))
    )
    for step in range(ITERS):
        if step > 0:
            x = from_x(own)
            z = from_z(own)
        sent = far_rows(far_mask, own, x, far0, corner, far1)
        given = to_z(sent)
        held = near_rows(own_mask, own, x, z, near0, near1, far0, far1)
        if step == 0:
            image, own, gram = join(held, given, root)
        else:
            image, own, gram = advance(total, held, given, root)
        total = total_sum(gram, step == ITERS - 1)
    return solve(total, image).T


def solution(mesh):
    in_specs = (P(("row", "col"), None), P(("row", "col"), None), P(("row", "col"), None))
    out_specs = P(("row", "col"), None)
    return jax.shard_map(on_device, mesh=mesh, in_specs=in_specs, out_specs=out_specs, check_vma=False)
```

```python
import functools
import math

import jax
import jax.numpy as jnp
from jax import lax
from jax.experimental import pallas as pl
from jax.experimental.pallas import tpu as pltpu
from jax.sharding import PartitionSpec as P

REACH = 2
ITERS = 3
BLK_DEV = 2

SHARP = 8.0
EPSILON = 1e-06

F32 = jnp.float32
BF16 = jnp.bfloat16
EXACT = lax.Precision.HIGHEST
VMEM = pl.BlockSpec(memory_space=pltpu.VMEM)
SMEM = pl.BlockSpec(memory_space=pltpu.SMEM)


def call(body, out_shape, in_specs, flops, moved, room=6):
    return pl.pallas_call(
        body,
        out_shape=out_shape,
        in_specs=in_specs,
        out_specs=jax.tree.map(lambda _: VMEM, out_shape),
        cost_estimate=pl.CostEstimate(flops=flops, bytes_accessed=moved, transcendentals=0),
        compiler_params=pltpu.CompilerParams(vmem_limit_bytes=room << 20),
    )


def shaped(shape, dtype):
    return jax.ShapeDtypeStruct(shape, dtype)


def cross(left, right, **kw):
    return lax.dot_general(
        left, right, (((1,), (1,)), ((), ())), preferred_element_type=F32, **kw
    )


STEPS = 8


def unit_rows_body(first, points_ref, out_ref, held, arrived):
    size = out_ref.shape[0]
    step = size // STEPS
    copies = []
    for at in range(STEPS):
        rows = pl.ds(at * step, step)
        source = points_ref.at[pl.ds(first + at * step, step)]
        copies.append(pltpu.make_async_copy(source, held.at[rows], arrived.at[at]))
        copies[-1].start()
    for at in range(STEPS):
        copies[at].wait()
        rows = pl.ds(at * step, step)
        points = held[rows, :]
        mean = jnp.mean(points * points, axis=-1, keepdims=True)
        out_ref[rows, :] = (points * lax.rsqrt(mean + EPSILON)).astype(BF16)


def unit_rows(points, first, size):
    width = points.shape[1]
    return pl.pallas_call(
        functools.partial(unit_rows_body, first),
        in_specs=[pl.BlockSpec(memory_space=pltpu.HBM)],
        out_specs=VMEM,
        out_shape=shaped((size, width), BF16),
        scratch_shapes=[pltpu.VMEM((size, width), F32), pltpu.SemaphoreType.DMA((STEPS,))],
        cost_estimate=pl.CostEstimate(
            flops=3 * size * width, bytes_accessed=6 * size * width, transcendentals=0
        ),
        compiler_params=pltpu.CompilerParams(vmem_limit_bytes=4 << 20),
        name="unit_rows",
    )(pltpu.with_memory_space_constraint(points, pltpu.HBM))


def affinity(rows, cols):
    width = rows.shape[1]
    return jnp.exp(cross(rows, cols) * (SHARP / width) - SHARP)


def down(tile):
    return jnp.sum(tile, axis=0, keepdims=True)


def across(tile):
    lanes = 128
    folded = tile[:, :lanes]
    for at in range(lanes, tile.shape[1], lanes):
        folded = folded + tile[:, at : at + lanes]
    return jnp.sum(folded.T, axis=0, keepdims=True)


def gated(mask, sums):
    return jnp.where(mask > 0.0, sums, 0.0)


def span(index, size):
    return slice(index * size, (index + 1) * size)


def pieces(part, block, start, size):
    found = []
    at = 0
    while at < part.shape[0]:
        inside = (start + at) % size
        count = min(size - inside, part.shape[0] - at)
        index = block + (start + at) // size
        found.append((part[at : at + count, :], index, slice(start + at, start + at + count)))
        at += count
    return found


def shifted(where, by):
    return slice(where.start + by, where.stop + by)


def near_tiles(own_mask, rows, cols, near, base, degree):
    for left, l, down_at in rows:
        for right, m, at in cols:
            tile = affinity(left, right)
            near[shifted(down_at, base), at] = tile.astype(BF16)
            degree[:, at] += gated(own_mask[m, l], down(tile))


def far_tiles(own_mask, rows, cols, far, by, degree, sums):
    for left, l, down_at in rows:
        for right, m, at in cols:
            tile = affinity(left, right)
            far[shifted(down_at, by[0]), shifted(at, by[1])] = tile.astype(BF16)
            sums[l : l + 1, shifted(at, by[1])] += down(tile)
            if l < BLK_DEV:
                degree[:, down_at] += gated(own_mask[l, 2 * BLK_DEV + m], across(tile))


def first_tiles_body(own_mask, pa, pb, xa, za, near, far, degree, sums):
    most, points = pa.shape[0], near.shape[1]
    size = points // BLK_DEV
    degree[...] = jnp.zeros_like(degree)
    sums[...] = jnp.zeros_like(sums)
    own = pieces(pa, 0, 0, size) + pieces(pb, 0, most, size)
    side = pieces(xa, BLK_DEV, 0, size)
    away = pieces(za, 0, 0, size)
    near_tiles(own_mask, own, own, near, 0, degree)
    near_tiles(own_mask, side, own, near, points, degree)
    far_tiles(own_mask, own, away, far, (0, 0), degree, sums)
    far_tiles(own_mask, side, away, far, (points, 0), degree, sums)


def last_tiles_body(
    own_mask, far_mask, pa, pb, xa, xb, za, zb, degree_in, sums_in,
    near, corner, far, degree, far_degree, sums, late,
):
    most, points = pa.shape[0], near.shape[1]
    size = points // BLK_DEV
    degree[...] = degree_in[...]
    sums[...] = sums_in[...]
    late[...] = jnp.zeros_like(late)
    own = pieces(pa, 0, 0, size) + pieces(pb, 0, most, size)
    side, rest = pieces(xa, BLK_DEV, 0, size), pieces(xb, BLK_DEV, most, size)
    away, final = pieces(za, 0, 0, size), pieces(zb, 0, most, size)
    near_tiles(own_mask, rest, own, near, -most, degree)
    far_tiles(own_mask, rest, away, corner, (-most, 0), degree, sums)
    far_tiles(own_mask, own, final, far, (0, -most), degree, late)
    far_tiles(own_mask, side + rest, final, far, (points, -most), degree, late)
    for cols, source, by in ((away, sums, 0), (final, late, -most)):
        for _, m, at in cols:
            total = jnp.zeros((1, at.stop - at.start), F32)
            for l in range(2 * BLK_DEV):
                total += gated(far_mask[m, l], source[l : l + 1, shifted(at, by)])
            far_degree[:, at] = total


def bfloat_rows(value):
    if value.dtype == BF16:
        return value
    high = value.astype(BF16)
    rest = value - high.astype(F32)
    middle = rest.astype(BF16)
    low = (rest - middle.astype(F32)).astype(BF16)
    return jnp.concatenate([high, middle, low], axis=0)


def whole_rows(value, count):
    if value.shape[0] == count:
        return value
    return (value[2 * count :] + value[count : 2 * count]) + value[:count]


def kept(mask, m, first, *vectors):
    parts = []
    at = first
    for value in vectors:
        size = value.shape[1] // BLK_DEV
        for l in range(BLK_DEV):
            part = value[:, span(l, size)]
            parts.append(jnp.where(mask[m, at] > 0.0, part, jnp.zeros_like(part)))
            at += 1
    return jnp.concatenate(parts, axis=1)


def apart(left, right):
    return jnp.dot(left, right, preferred_element_type=F32)


def far_rows_body(mask, own_ref, x_ref, far0, corner, far1, out):
    own, x = bfloat_rows(own_ref[...]), bfloat_rows(x_ref[...])
    count, points = out.shape
    size = points // BLK_DEV
    cut, most = far0.shape
    for m in range(BLK_DEV):
        left = kept(mask, m, 0, own, x)
        there = slice(m * size, min((m + 1) * size, most))
        total = apart(left[:, :cut], far0[:, there]) + apart(left[:, cut:], corner[:, there])
        out[:, there] = whole_rows(total, count)
    out[:, most:] = whole_rows(apart(left, far1[...]), count)


def near_rows_body(mask, own_ref, x_ref, z_ref, near0, near1, far0, far1, out):
    own, x, z = bfloat_rows(own_ref[...]), bfloat_rows(x_ref[...]), bfloat_rows(z_ref[...])
    size = own.shape[1] // BLK_DEV
    cut, most = far0.shape
    for m in range(BLK_DEV):
        there = span(m, size)
        left = kept(mask, m, 0, own, x)
        side = kept(mask, m, 2 * BLK_DEV, z)
        total = apart(left[:, :cut], near0[:, there]) + apart(left[:, cut:], near1[:, there])
        total += cross(side[:, :most], far0[there, :]) + cross(side[:, most:], far1[there, :])
        out[:, there] = whole_rows(total, out.shape[0])


def finish(full, root, image, ahead, gram):
    image[...] = full
    ahead[...] = full * root[...]
    gram[...] = cross(full, full, precision=EXACT)


def join_body(near, given, root, image, ahead, gram):
    finish((near[...] + given[...]) * root[...], root, image, ahead, gram)


def advance_body(scale, total, near, given, root, image, ahead, gram):
    factor = inverse_factor(total[...]) * scale
    full = (near[...] + given[...]) * root[...]
    solved = jnp.dot(factor, full, preferred_element_type=F32, precision=EXACT)
    finish(solved, root, image, ahead, gram)


GROUP = 8


def inverse_factor(gram):
    size = gram.shape[0]
    rows = lax.broadcasted_iota(jnp.int32, (size, 2 * size), 0)
    lanes = lax.broadcasted_iota(jnp.int32, (size, 2 * size), 1)
    unit = jnp.where(rows + size == lanes, 1.0, 0.0).astype(F32)
    live = jnp.concatenate([gram, unit[:, size:]], axis=1)
    finished = []
    for first in range(0, size, GROUP):
        cols = [
            jnp.broadcast_to(live[:, first + b : first + b + 1], live.shape) for b in range(GROUP)
        ]
        lines = [live[a : a + 1, :] for a in range(GROUP)]
        pivots = {(a, b): cols[b][a : a + 1, :] for a in range(GROUP) for b in range(a, GROUP)}
        change = jnp.zeros_like(live)
        for a in range(GROUP):
            inverse = 1.0 / pivots[a, a]
            for b in range(a + 1, GROUP):
                ratio = pivots[a, b] * inverse
                lines[b] = lines[b] - ratio * lines[a]
                cols[b] = cols[b] - ratio * cols[a]
                for c in range(b, GROUP):
                    pivots[b, c] = pivots[b, c] - ratio * pivots[a, c]
            change += cols[a] * inverse * lines[a]
            finished.append(lines[a] * lax.rsqrt(pivots[a, a]))
        if first + GROUP < size:
            live = (live - change)[GROUP:, :]
    return jnp.concatenate(finished, axis=0)[:, size:]


def solve_body(scale, total, image, out):
    factor = inverse_factor(total[...]) * scale
    out[...] = jnp.dot(factor, image[...], preferred_element_type=F32, precision=EXACT)


def exchange_masks(row_count, col_count, alone):
    low = [1 << bit for bit in range(col_count.bit_length() - 1)]
    high = [col_count << bit for bit in range(row_count.bit_length() - 1)]
    if alone:
        stages = [(high[0],), (high[1], low[0]), (low[1], low[2])]
    else:
        stages = [(low[1], low[2]), (high[0], high[1]), (low[0],)]
    rest = high[2:] + low[3:]
    return stages + [tuple(rest[at : at + 2]) for at in range(0, len(rest), 2)]


def total_sum(value, alone):
    row_count = lax.axis_size("row")
    col_count = lax.axis_size("col")
    devices = row_count * col_count
    if devices & (devices - 1) or row_count < 4 or col_count < 8:
        return lax.psum(value, ("row", "col"))

    def fetched(mask):
        pairs = [(source, source ^ mask) for source in range(devices)]
        return lax.ppermute(value, ("row", "col"), pairs)

    for masks in exchange_masks(row_count, col_count, alone):
        if len(masks) == 1:
            value = value + fetched(masks[0])
        else:
            first, second = masks
            near, far, both = fetched(first), fetched(second), fetched(first ^ second)
            value = (value + near) + (far + both)
    return value


def listed(ids, blocks):
    found = jnp.zeros((ids.shape[0], blocks.shape[0]), bool)
    for slot in range(ids.shape[1]):
        found = found | (ids[:, slot : slot + 1] == blocks[None, :])
    return found.astype(F32)


def on_device(embeddings, neighbour_ids, start_vectors):
    col_count = lax.axis_size("col")
    col = lax.axis_index("col")
    base = lax.axis_index("row") * col_count
    points, width = embeddings.shape
    columns = start_vectors.shape[1]
    size = points // BLK_DEV
    total_rows = points * lax.axis_size("row") * col_count

    def side_of(index):
        return (index + (REACH if index % 2 == 0 else -REACH)) % col_count

    def from_x(value):
        return lax.ppermute(value, "col", [(i, i ^ 1) for i in range(col_count)])

    def from_z(value):
        return lax.ppermute(value, "col", [(side_of(i), i) for i in range(col_count)])

    def to_z(value):
        return lax.ppermute(value, "col", [(i, side_of(i)) for i in range(col_count)])

    def to_z_side(value):
        return lax.ppermute(value, "col", [(i, side_of(i) ^ 1) for i in range(col_count)])

    most = points - size // 2
    b0 = unit_rows(embeddings, 0, most)
    z0 = from_z(b0)
    x0 = from_x(b0)
    b1 = unit_rows(embeddings, most, points - most)
    z1 = from_z(b1)
    x1 = from_x(b1)
    far_ids = from_z(neighbour_ids)
    start = start_vectors.T
    start_x = from_x(start)
    start_z = from_z(start)

    here = base + col
    x_side = base + (col ^ 1)
    z_side = base + (col + jnp.where(col % 2 == 0, REACH, col_count - REACH)) % col_count
    members = jnp.arange(BLK_DEV, dtype=jnp.int32)
    nearby = jnp.stack([here, x_side, z_side])[:, None] * BLK_DEV + members[None, :]
    nearby = nearby.reshape(-1)
    own_mask = listed(neighbour_ids, nearby)
    far_mask = listed(far_ids, nearby[: 2 * BLK_DEV])

    line = shaped((1, points), F32)
    one = 2 * size * size * width
    moved = 4 * size * width
    tall, less = points + most, points - most
    near0, far0, degree, sums = call(
        first_tiles_body,
        (
            shaped((tall, points), BF16), shaped((tall, most), BF16), line,
            shaped((2 * BLK_DEV, most), F32),
        ),
        [SMEM] + [VMEM] * 4, 12 * one, 12 * moved, room=14,
    )(own_mask, b0, b1, x0, z0)
    near1, corner, far1, degree, far_degree, _, _ = call(
        last_tiles_body,
        (
            shaped((less, points), BF16), shaped((less, most), BF16),
            shaped((2 * points, less), BF16), line, line,
            shaped((2 * BLK_DEV, most), F32), shaped((2 * BLK_DEV, less), F32),
        ),
        [SMEM] * 2 + [VMEM] * 8, 4 * one, 4 * moved, room=14,
    )(own_mask, far_mask, b0, b1, x0, x1, z0, z1, degree, sums)
    root = lax.rsqrt(degree + to_z(far_degree))
    root_x = lax.rsqrt(from_x(degree) + to_z_side(far_degree))
    root_z = lax.rsqrt(from_z(degree) + far_degree)

    across_shape = (columns, points)
    work = 2 * columns * size * size
    wide = shaped(across_shape, F32)
    far_rows = call(far_rows_body, wide, [SMEM] + [VMEM] * 5, 8 * work, 8 * work // 64)
    near_rows = call(near_rows_body, wide, [SMEM] + [VMEM] * 7, 12 * work, 12 * work // 64)
    results = (wide, wide, shaped((columns, columns), F32))
    effort = 2 * columns * columns * points, 4 * columns * points
    scale = math.sqrt(total_rows)
    join = call(join_body, results, [VMEM] * 3, *effort)
    advance = call(functools.partial(advance_body, scale), results, [VMEM] * 4, *effort)
    solve = call(functools.partial(solve_body, scale), wide, [VMEM] * 2, *effort)

    own, x, z = (
        (value * line).astype(BF16)
        for value, line in ((start, root), (start_x, root_x), (start_z, root_z))
    )
    for step in range(ITERS):
        if step > 0:
            x = from_x(own)
            z = from_z(own)
        sent = far_rows(far_mask, own, x, far0, corner, far1)
        given = to_z(sent)
        held = near_rows(own_mask, own, x, z, near0, near1, far0, far1)
        if step == 0:
            image, own, gram = join(held, given, root)
        else:
            image, own, gram = advance(total, held, given, root)
        total = total_sum(gram, step == ITERS - 1)
    return solve(total, image).T


def solution(mesh):
    in_specs = (P(("row", "col"), None), P(("row", "col"), None), P(("row", "col"), None))
    out_specs = P(("row", "col"), None)
    return jax.shard_map(on_device, mesh=mesh, in_specs=in_specs, out_specs=out_specs, check_vma=False)
```
